32 devices in a mesh: shard: 4 (over x, core), rep: 8 (over z, y).
Axes of the slice: x: 2, y: 2, z: 4, core: 2. Of those that a mesh axis runs over, the one named last changes fastest.
Arguments:
- block_input: bfloat16 [8, 512, 768], P('rep', 'shard'), may hold values from -6 to 6
- positions: int32 [8, 512], P('rep', 'shard'), may hold values from 0 to 1022, as said below
- segments: int32 [8, 512], P('rep'), may hold values from 0 to 6, as said below
- w_qkv: bfloat16 [768, 2304], P('shard')
- b_qkv: bfloat16 [2304], P('shard'), may hold values from -3 to 3
- w_out: bfloat16 [768, 768], P('shard'), may hold values from -0.875 to 0.875
- b_out: bfloat16 [768], P('shard'), may hold values from -3 to 3
- w_up: bfloat16 [768, 3072], P('shard'), may hold values from -0.21875 to 0.21875
- b_up: bfloat16 [3072], P('shard'), may hold values from -3 to 3
- w_down: bfloat16 [3072, 768], P('shard'), may hold values from -0.109375 to 0.109375
- b_down: bfloat16 [768], P('shard'), may hold values from -3 to 3
- ln1_gain: bfloat16 [768], P('shard'), may hold values from 0.5 to 1.5
- ln1_bias: bfloat16 [768], P('shard'), may hold values from -2 to 2
- ln2_gain: bfloat16 [768], P('shard'), may hold values from 0.5 to 1.5
- ln2_bias: bfloat16 [768], P('shard'), may hold values from -2 to 2
- cotangent: bfloat16 [8, 512, 768], P('rep', 'shard'), may hold values from -6 to 6
Outputs:
- output: float32 [8, 512, 768], P('rep', 'shard')
- input_grad: float32 [8, 512, 768], P('rep', 'shard')
- grad_w_qkv: float32 [768, 2304], P('shard')
- grad_b_qkv: float32 [2304], P('shard')
- grad_w_out: float32 [768, 768], P('shard')
- grad_b_out: float32 [768], P('shard')
- grad_w_up: float32 [768, 3072], P('shard')
- grad_b_up: float32 [3072], P('shard')
- grad_w_down: float32 [3072, 768], P('shard')
- grad_b_down: float32 [768], P('shard')
- grad_ln1_gain: float32 [768], P('shard')
- grad_ln1_bias: float32 [768], P('shard')
- grad_ln2_gain: float32 [768], P('shard')
- grad_ln2_bias: float32 [768], P('shard')
The draws below stay inside these ranges and needn't reach their ends.
Inputs may be any that keep to these rules, and one draw needn't show every extreme that they name: `segments`: a token's document number within its sequence: 0 at the sequence's first token, one more at each document start; every document that starts inside a sequence has 102 tokens or more. `positions`: a token's position within its document, one more than that of the token before it inside the same document, 0 at a document's first token; a sequence's first document may have begun in an earlier sequence.
All inputs are finite; a program needn't handle non-finite values.
Results may differ from the reference program's by a relative error of at most 0.011.
Values may be sent and summed in bfloat16 or wider, within the bound.
No kernel may reach another device: no remote copies, remote signals or barrier semaphores. Data moves between devices by JAX's collectives and lax.ppermute only.
A program may use at most 128 MiB of HBM per device.

```python
import math
import jax
import jax.numpy as jnp
from jax import lax

D = 768
HEADS = 12
HEAD_DIM = 64
ROT = 16
FF = 3072
LEN = 512
SEQS = 8


def doc_layout(key):
    base = jax.random.fold_in(key, 11)
    shortest = LEN // 5
    lengths = jax.random.randint(jax.random.fold_in(base, 1), (SEQS, 7), shortest, 2 * LEN)
    offsets = jax.random.randint(jax.random.fold_in(base, 2), (SEQS,), 0, lengths[:, 0])
    row_ids = jnp.arange(SEQS)[:, None]
    column_ids = jnp.arange(7)[None, :]
    lengths = jnp.where(row_ids == 0, shortest, lengths)
    lengths = jnp.where((row_ids == 1) & (column_ids == 0), 2 * LEN - 1, lengths)
    offsets = jnp.where(row_ids[:, 0] == 0, shortest - 1, offsets)
    offsets = jnp.where(row_ids[:, 0] == 1, LEN - 1, offsets)
    ends = jnp.cumsum(lengths, axis=1) - offsets[:, None]
    places = jnp.arange(LEN)
    segment = jnp.sum((ends[:, None, :] <= places[None, :, None]).astype(jnp.int32), axis=2)
    starts = jnp.concatenate([-offsets[:, None], ends[:, :-1]], axis=1)
    position = places[None, :] - jnp.take_along_axis(starts, segment, axis=1)
    return (segment.astype(jnp.int32), position.astype(jnp.int32))


def draw_segments(key, part):
    return doc_layout(key)[0]


def draw_positions(key, part):
    return doc_layout(key)[1]


def draw_w_qkv(key, part):
    base = jax.random.normal(jax.random.fold_in(key, 3), (D, 3 * D), jnp.float32) * D ** (-0.5)
    return base.astype(jnp.bfloat16)


def block_scale(own_key, shape, split, smallest, top_value):
    level = 1.0
    for dim, blocks in split:
        steps = jax.random.uniform(jax.random.fold_in(jax.random.fold_in(own_key, 6), dim), (blocks,), jnp.float32, smallest / len(split), top_value / len(split))
        level = level * jnp.repeat(jnp.exp(steps), shape[dim] // blocks).reshape((-1,) + (1,) * (len(shape) - 1 - dim))
    return level


def bell_draw(own_key, dims, spread, reach, cuts=(), held_as=jnp.bfloat16):
    entries = spread * jax.random.normal(own_key, dims, jnp.float32)
    if cuts:
        entries = entries * block_scale(own_key, dims, cuts, -0.22, 0.18)
    return jnp.clip(entries, -reach, reach).astype(held_as)


def setup_inputs(seed: int = 0) -> dict:
    splits = jax.random.split(jax.random.key(seed), 17)
    block_input = bell_draw(splits[0], (SEQS, LEN, D), 1.0, 6.0, ((0, 8), (1, 4)))
    positions = draw_positions(jax.random.fold_in(splits[16], 71), 0)
    segments = draw_segments(jax.random.fold_in(splits[16], 71), 0)
    w_qkv = draw_w_qkv(jax.random.fold_in(splits[16], 71), 0)
    b_qkv = bell_draw(splits[4], (3 * D,), 0.5, 3.0, ((0, 4),))
    w_out = bell_draw(splits[5], (D, D), (D // 16) ** -0.5, 0.875, ((0, 4),))
    b_out = bell_draw(splits[6], (D,), 0.5, 3.0, ((0, 4),))
    w_up = bell_draw(splits[7], (D, FF), D ** -0.5, 0.21875, ((0, 4),))
    b_up = bell_draw(splits[8], (FF,), 0.5, 3.0, ((0, 4),))
    w_down = bell_draw(splits[9], (FF, D), FF ** -0.5, 0.109375, ((0, 4),))
    b_down = bell_draw(splits[10], (D,), 0.5, 3.0, ((0, 4),))
    ln1_gain = jnp.clip(1.0 + 0.1 * jax.random.normal(splits[11], (D,), jnp.float32), 0.5, 1.5).astype(jnp.bfloat16)
    ln1_bias = bell_draw(splits[12], (D,), 0.3, 2.0, ((0, 4),))
    ln2_gain = jnp.clip(1.0 + 0.1 * jax.random.normal(splits[13], (D,), jnp.float32), 0.5, 1.5).astype(jnp.bfloat16)
    ln2_bias = bell_draw(splits[14], (D,), 0.3, 2.0, ((0, 4),))
    cotangent = bell_draw(splits[15], (SEQS, LEN, D), 1.0, 6.0, ((0, 8), (1, 4)))
    return dict(block_input=block_input, positions=positions, segments=segments, w_qkv=w_qkv, b_qkv=b_qkv, w_out=w_out, b_out=b_out, w_up=w_up, b_up=b_up, w_down=w_down, b_down=b_down, ln1_gain=ln1_gain, ln1_bias=ln1_bias, ln2_gain=ln2_gain, ln2_bias=ln2_bias, cotangent=cotangent)


EPSILON = 1e-05
INV_ROOT_TWO = 0.7071067811865476
INV_ROOT_TWO_PI = 0.3989422804014327

def as_float(array_in):
    return array_in.astype(jnp.float32)

def normalize(values):
    centre = values - lax.optimization_barrier(jnp.mean(values, axis=-1, keepdims=True))
    inv_std = lax.rsqrt(lax.optimization_barrier(jnp.mean(centre * centre, axis=-1, keepdims=True)) + EPSILON)
    return (centre * inv_std, inv_std)

def rotary_tables(position):
    half = ROT // 2
    index_f = jnp.arange(half).astype(jnp.float32)
    freqs = jnp.exp(index_f * (-math.log(10000.0) / half))
    angles = position.astype(jnp.float32)[:, None] * freqs[None, :]
    return (jnp.cos(angles), jnp.sin(angles))

def rotate(heads_in, cosine, sine, direction):
    half = ROT // 2
    first = heads_in[..., :half]
    second = heads_in[..., half:ROT]
    cos_b = cosine[:, None, :]
    sin_b = direction * sine[:, None, :]
    return jnp.concatenate([first * cos_b - second * sin_b, second * cos_b + first * sin_b, heads_in[..., ROT:]], axis=-1)

def gelu_value(pre_act):
    return 0.5 * pre_act * (1.0 + jax.scipy.special.erf(pre_act * INV_ROOT_TWO))

def gelu_slope(pre_act):
    return 0.5 * (1.0 + jax.scipy.special.erf(pre_act * INV_ROOT_TWO)) + pre_act * jnp.exp(-0.5 * pre_act * pre_act) * INV_ROOT_TWO_PI

def layer_pass(params, tokens_in, cotan, position, segment):
    w_qkv, b_qkv, w_out, b_out, w_up, b_up, w_down, b_down, gain_one, bias_one, gain_two, bias_two = params
    count = tokens_in.shape[0]
    resid = as_float(tokens_in)
    normed, inv_std = normalize(resid)
    hid_one = (normed * as_float(gain_one) + as_float(bias_one)).astype(jnp.bfloat16)
    hid_two = (normed * as_float(gain_two) + as_float(bias_two)).astype(jnp.bfloat16)
    projected = jnp.dot(hid_one, w_qkv, preferred_element_type=jnp.float32) + as_float(b_qkv)
    queries = projected[:, :D].reshape(count, HEADS, HEAD_DIM)
    keys_raw = projected[:, D:2 * D].reshape(count, HEADS, HEAD_DIM)
    cosine, sine = rotary_tables(position)
    query_rot = rotate(queries, cosine, sine, 1.0).astype(jnp.bfloat16)
    key_rot = rotate(keys_raw, cosine, sine, 1.0).astype(jnp.bfloat16)
    value_b = projected[:, 2 * D:].reshape(count, HEADS, HEAD_DIM).astype(jnp.bfloat16)
    places = jnp.arange(count)
    allowed = (places[None, :] <= places[:, None]) & (segment[:, None] == segment[None, :])
    scores = jnp.einsum('qhd,khd->hqk', as_float(query_rot), as_float(key_rot)) * 0.125
    scores = jnp.where(allowed[None], scores, -jnp.inf)
    top = lax.optimization_barrier(jnp.max(scores, axis=-1, keepdims=True))
    log_total = top + jnp.log(lax.optimization_barrier(jnp.sum(jnp.exp(scores - top), axis=-1, keepdims=True)))
    attn_prob = jnp.exp(scores - log_total)
    prob_b = attn_prob.astype(jnp.bfloat16)
    attended_h = jnp.einsum('hqk,khd->qhd', as_float(prob_b), as_float(value_b)).astype(jnp.bfloat16)
    attended = attended_h.reshape(count, D)
    branch_attn = jnp.dot(attended, w_out, preferred_element_type=jnp.float32) + as_float(b_out)
    pre_act = jnp.dot(hid_two, w_up, preferred_element_type=jnp.float32) + as_float(b_up)
    activ = gelu_value(pre_act).astype(jnp.bfloat16)
    branch_mlp = jnp.dot(activ, w_down, preferred_element_type=jnp.float32) + as_float(b_down)
    output = resid + branch_attn + branch_mlp
    cot_f = as_float(cotan)
    grad_b_down = lax.optimization_barrier(jnp.sum(cot_f, axis=0))
    grad_w_down = jnp.dot(activ.T, cotan, preferred_element_type=jnp.float32)
    d_activ = jnp.dot(cotan, w_down.T, preferred_element_type=jnp.float32)
    d_pre = d_activ * gelu_slope(pre_act)
    d_pre_b = d_pre.astype(jnp.bfloat16)
    grad_b_up = lax.optimization_barrier(jnp.sum(d_pre, axis=0))
    grad_w_up = jnp.dot(hid_two.T, d_pre_b, preferred_element_type=jnp.float32)
    d_hid_two = jnp.dot(d_pre_b, w_up.T, preferred_element_type=jnp.float32)
    grad_b_out = lax.optimization_barrier(jnp.sum(cot_f, axis=0))
    grad_w_out = jnp.dot(attended.T, cotan, preferred_element_type=jnp.float32)
    d_att = jnp.dot(cotan, w_out.T, preferred_element_type=jnp.float32).astype(jnp.bfloat16).reshape(count, HEADS, HEAD_DIM)
    d_value = jnp.einsum('hqk,qhd->khd', as_float(prob_b), as_float(d_att))
    d_prob = jnp.einsum('qhd,khd->hqk', as_float(d_att), as_float(value_b))
    row_dot = lax.optimization_barrier(jnp.sum(as_float(d_att) * as_float(attended_h), axis=-1)).T[:, :, None]
    d_score = attn_prob * (d_prob - row_dot)
    d_score_b = (d_score * 0.125).astype(jnp.bfloat16)
    d_qrot = jnp.einsum('hqk,khd->qhd', as_float(d_score_b), as_float(key_rot))
    d_krot = jnp.einsum('hqk,qhd->khd', as_float(d_score_b), as_float(query_rot))
    d_query = rotate(d_qrot, cosine, sine, -1.0)
    d_key = rotate(d_krot, cosine, sine, -1.0)
    d_proj = jnp.concatenate([d_query.reshape(count, D), d_key.reshape(count, D), d_value.reshape(count, D)], axis=1)
    grad_b_qkv = lax.optimization_barrier(jnp.sum(d_proj, axis=0))
    d_proj_b = d_proj.astype(jnp.bfloat16)
    grad_w_qkv = jnp.dot(hid_one.T, d_proj_b, preferred_element_type=jnp.float32)
    d_hid_one = jnp.dot(d_proj_b, w_qkv.T, preferred_element_type=jnp.float32)
    grad_gain_one = lax.optimization_barrier(jnp.sum(d_hid_one * normed, axis=0))
    grad_bias_one = lax.optimization_barrier(jnp.sum(d_hid_one, axis=0))
    grad_gain_two = lax.optimization_barrier(jnp.sum(d_hid_two * normed, axis=0))
    grad_bias_two = lax.optimization_barrier(jnp.sum(d_hid_two, axis=0))
    d_norm = d_hid_one * as_float(gain_one) + d_hid_two * as_float(gain_two)
    d_input = cot_f + inv_std * (d_norm - lax.optimization_barrier(jnp.mean(d_norm, axis=-1, keepdims=True)) - normed * lax.optimization_barrier(jnp.mean(d_norm * normed, axis=-1, keepdims=True)))
    grads = (grad_w_qkv, grad_b_qkv, grad_w_out, grad_b_out, grad_w_up, grad_b_up, grad_w_down, grad_b_down, grad_gain_one, grad_bias_one, grad_gain_two, grad_bias_two)
    return (output, d_input, grads)

def reference(block_input, positions, segments, w_qkv, b_qkv, w_out, b_out, w_up, b_up, w_down, b_down, ln1_gain, ln1_bias, ln2_gain, ln2_bias, cotangent):
    params = (w_qkv, b_qkv, w_out, b_out, w_up, b_up, w_down, b_down, ln1_gain, ln1_bias, ln2_gain, ln2_bias)
    zeros = tuple((jnp.zeros(param.shape, jnp.float32) for param in params))

    def one_sequence(totals, inputs):
        seq_input, dy_seq, pos_seq, seg_seq = inputs
        out_seq, dx_seq, grads = layer_pass(params, seq_input, dy_seq, pos_seq, seg_seq)
        return (tuple((total + grad for total, grad in zip(totals, grads))), (out_seq, dx_seq))
    totals, (outputs, input_grad) = lax.scan(one_sequence, zeros, (block_input, cotangent, positions, segments))
    return (outputs, input_grad, totals[0], totals[1], totals[2], totals[3], totals[4], totals[5], totals[6], totals[7], totals[8], totals[9], totals[10], totals[11])
```

```python
import math

import jax
import jax.numpy as jnp
from jax import lax
from jax.sharding import PartitionSpec as P

HEAD_DIM = 64
ROT = 16

EPSILON = 1e-05
INV_ROOT_TWO = 0.7071067811865476
INV_ROOT_TWO_PI = 0.3989422804014327


BF = jnp.bfloat16
F32 = jnp.float32


def as_float(array_in):
    return array_in.astype(F32)


def dot(left, right, dims):
    return lax.dot_general(left, right, (dims, ((), ())), preferred_element_type=F32)


def normalize(values):
    centre = values - jnp.mean(values, axis=-1, keepdims=True)
    inv_std = lax.rsqrt(jnp.mean(centre * centre, axis=-1, keepdims=True) + EPSILON)
    return (centre * inv_std, inv_std)


def rotary_tables(position):
    half = ROT // 2
    index_f = jnp.arange(half).astype(F32)
    freqs = jnp.exp(index_f * (-math.log(10000.0) / half))
    angles = position.astype(F32)[:, None] * freqs[None, :]
    return (jnp.cos(angles), jnp.sin(angles))


def rotate(heads_in, cosine, sine, direction):
    half = ROT // 2
    first = heads_in[..., :half]
    second = heads_in[..., half:ROT]
    cos_b = cosine[:, None, :]
    sin_b = direction * sine[:, None, :]
    return jnp.concatenate(
        [first * cos_b - second * sin_b, second * cos_b + first * sin_b, heads_in[..., ROT:]],
        axis=-1,
    )


def gelu_value(pre_act):
    return 0.5 * pre_act * (1.0 + jax.scipy.special.erf(pre_act * INV_ROOT_TWO))


def gelu_slope(pre_act):
    return (
        0.5 * (1.0 + jax.scipy.special.erf(pre_act * INV_ROOT_TWO))
        + pre_act * jnp.exp(-0.5 * pre_act * pre_act) * INV_ROOT_TWO_PI
    )


def swap(value, axis, size, bit):
    return lax.ppermute(value, axis, [(i, i ^ bit) for i in range(size)])


def powers(size):
    return [1 << k for k in range(size.bit_length() - 1)]


def cube_gather(value, axis, size):
    buf, order = value[None], [0]
    for bit in reversed(powers(size)):
        buf = jnp.concatenate([buf, swap(buf, axis, size, bit)])
        order = order + [j ^ bit for j in order]
    return buf, order


def cube_scatter(value, axis, size):
    for bit in powers(size):
        half = value.shape[0] // 2
        got = swap(value[half:], axis, size, bit)
        total = as_float(value[:half]) + as_float(got)
        value = total.astype(value.dtype) if half > 1 else total
    return value[0]


def absolute(blocks, order, me):
    place = {off: k for k, off in enumerate(order)}
    table = jnp.array([place[i] for i in range(len(order))], jnp.int32)
    idx = table[jnp.arange(len(order)) ^ me]
    return jnp.stack([lax.dynamic_index_in_dim(blocks, idx[i], 0, False) for i in range(len(order))])


def halve(value, axis, me, size, bit):
    n = value.shape[axis] // 2
    up = (me & bit) != 0
    keep = lax.dynamic_slice_in_dim(value, jnp.where(up, n, 0), n, axis)
    send = lax.dynamic_slice_in_dim(value, jnp.where(up, 0, n), n, axis)
    got = swap(send, "rep", size, bit)
    return (as_float(keep) + as_float(got)).astype(BF)


def double(value, axis, me, size, bit):
    got = swap(value, "rep", size, bit)
    up = (me & bit) != 0
    return jnp.where(
        up, jnp.concatenate([got, value], axis), jnp.concatenate([value, got], axis)
    )


def all_reduce(value, axes, bits, me, size, middle=None):
    at, change = middle if middle else (None, None)
    for k, bit in enumerate(bits):
        if k == at:
            value = change(value)
        value = halve(value, axes[k], me, size, bit)
    value = lax.optimization_barrier(value)
    for k in reversed(range(len(bits))):
        axis = 0 if middle and k < at else axes[k]
        value = double(value, axis, me, size, bits[k])
    return as_float(value)


def make_body(shards, reps):
    def body(
        block_input,
        positions,
        segments,
        w_qkv,
        b_qkv,
        w_out,
        b_out,
        w_up,
        b_up,
        w_down,
        b_down,
        ln1_gain,
        ln1_bias,
        ln2_gain,
        ln2_bias,
        cotangent,
    ):
        me = lax.axis_index("shard")
        mr = lax.axis_index("rep")
        tokens_in = block_input[0]
        cotan_own = cotangent[0]
        count, width = tokens_in.shape
        length = segments.shape[1]
        rows = w_qkv.shape[0]
        wide = w_up.shape[1] // shards
        heads = rows // HEAD_DIM

        position = positions[0]
        small = jnp.concatenate(
            [
                ln1_gain,
                ln1_bias,
                ln2_gain,
                ln2_bias,
                b_out,
                b_down,
                b_qkv,
                (position >> 5).astype(BF),
                (position & 31).astype(BF),
            ]
        )
        small_rel, order = cube_gather(small, "shard", shards)
        x_rel, _ = cube_gather(tokens_in, "shard", shards)
        c_rel, _ = cube_gather(cotan_own, "shard", shards)

        def exchange(piece):
            return absolute(
                jnp.stack(
                    [piece(me)] + [swap(piece(me ^ j), "shard", shards, j) for j in range(1, shards)]
                ),
                list(range(shards)),
                me,
            )

        up_full = exchange(
            lambda t: lax.dynamic_slice_in_dim(w_up, t * wide, wide, 1)
        ).reshape(width, wide)
        qkv3 = w_qkv.reshape(rows, 3, width)
        qkv_full = exchange(
            lambda t: lax.dynamic_slice_in_dim(qkv3, t * rows, rows, 2).reshape(rows, 3 * rows)
        ).reshape(width, 3 * rows)

        small_abs = absolute(small_rel, order, me)
        cuts = [0]
        for part in (rows, rows, rows, rows, rows, rows, 3 * rows, count, count):
            cuts.append(cuts[-1] + part)
        pieces = [small_abs[:, a:b] for a, b in zip(cuts[:-1], cuts[1:])]
        gain_one, bias_one, gain_two, bias_two, full_bout, full_bdown = [
            as_float(p.reshape(-1)) for p in pieces[:6]
        ]
        bias_qkv = as_float(
            lax.dynamic_slice_in_dim(pieces[6].reshape(3, width), me * rows, rows, 1).reshape(-1)
        )
        pos_rel = (
            small_rel[:, cuts[7] : cuts[8]].astype(jnp.int32) * 32
            + small_rel[:, cuts[8] : cuts[9]].astype(jnp.int32)
        ).reshape(-1)
        places = jnp.concatenate(
            [(me ^ j) * count + jnp.arange(count, dtype=jnp.int32) for j in order]
        )
        seg_abs = segments[0].reshape(shards, count)
        seg_rel = jnp.concatenate(
            [lax.dynamic_index_in_dim(seg_abs, me ^ j, 0, False) for j in order]
        )

        tokens = x_rel.reshape(length, width)
        cotan = c_rel.reshape(length, width)
        resid = as_float(tokens)
        normed, inv_std = normalize(resid)
        hid_two = (normed * gain_two + bias_two).astype(BF)
        hid_one = (normed * gain_one + bias_one).astype(BF)

        pre_act = dot(hid_two, up_full, ((1,), (0,))) + as_float(b_up)
        activ = gelu_value(pre_act).astype(BF)
        g_down = dot(activ, cotan, ((0,), (0,))).astype(BF)
        d_pre = dot(cotan, w_down, ((1,), (1,))) * gelu_slope(pre_act)
        d_pre_b = d_pre.astype(BF)
        g_up = dot(hid_two, d_pre_b, ((0,), (0,))).astype(BF)
        grad_bup = jnp.sum(d_pre, axis=0)
        part_mlp = dot(activ, w_down, ((1,), (0,)))
        d_hid_two = dot(d_pre_b, up_full, ((1,), (1,)))

        projected = dot(hid_one, qkv_full, ((1,), (0,))) + bias_qkv
        cosine, sine = rotary_tables(pos_rel)
        q_h = rotate(projected[:, :rows].reshape(length, heads, HEAD_DIM), cosine, sine, 1.0).astype(BF)
        k_h = rotate(
            projected[:, rows : 2 * rows].reshape(length, heads, HEAD_DIM), cosine, sine, 1.0
        ).astype(BF)
        v_h = projected[:, 2 * rows :].astype(BF).reshape(length, heads, HEAD_DIM)
        d_att = dot(cotan, w_out, ((1,), (1,))).astype(BF).reshape(length, heads, HEAD_DIM)
        allowed = (places[None, :] <= places[:, None]) & (seg_rel[:, None] == seg_rel[None, :])
        scores = jnp.einsum("qhd,khd->hqk", q_h, k_h, preferred_element_type=F32) * 0.125
        scores = jnp.where(allowed[None], scores, -jnp.inf)
        top = jnp.max(scores, axis=-1, keepdims=True)
        log_total = top + jnp.log(jnp.sum(jnp.exp(scores - top), axis=-1, keepdims=True))
        attn_prob = jnp.exp(scores - log_total)
        prob_b = attn_prob.astype(BF)
        att_h = jnp.einsum("hqk,khd->qhd", prob_b, v_h, preferred_element_type=F32).astype(BF)
        attended = att_h.reshape(length, rows)
        d_value = jnp.einsum("hqk,qhd->khd", prob_b, d_att, preferred_element_type=F32)
        d_prob = jnp.einsum("qhd,khd->hqk", d_att, v_h, preferred_element_type=F32)
        row_dot = jnp.sum(as_float(d_att) * as_float(att_h), axis=-1).T[:, :, None]
        d_score_b = (attn_prob * (d_prob - row_dot) * 0.125).astype(BF)
        d_qrot = jnp.einsum("hqk,khd->qhd", d_score_b, k_h, preferred_element_type=F32)
        d_krot = jnp.einsum("hqk,qhd->khd", d_score_b, q_h, preferred_element_type=F32)
        d_proj = jnp.concatenate(
            [
                rotate(d_qrot, cosine, sine, -1.0).reshape(length, rows),
                rotate(d_krot, cosine, sine, -1.0).reshape(length, rows),
                d_value.reshape(length, rows),
            ],
            axis=1,
        )
        d_proj_b = d_proj.astype(BF)
        g_out = dot(attended, cotan, ((0,), (0,))).astype(BF)
        g_qkv = dot(hid_one, d_proj_b, ((0,), (0,))).astype(BF)
        grad_bqkv = jnp.sum(d_proj, axis=0)
        d_hid_one = dot(d_proj_b, qkv_full, ((1,), (1,)))

        part_out = (dot(attended, w_out, ((1,), (0,))) + part_mlp).astype(BF)
        branch = cube_scatter(part_out.reshape(shards, count, width), "shard", shards)
        output = as_float(tokens_in) + branch + full_bout + full_bdown
        part_norm = (d_hid_one * gain_one + d_hid_two * gain_two).astype(BF)
        d_norm = cube_scatter(part_norm.reshape(shards, count, width), "shard", shards)
        own_normed = normed[:count]
        d_input = as_float(cotan_own) + inv_std[:count] * (
            d_norm
            - jnp.mean(d_norm, axis=-1, keepdims=True)
            - own_normed * jnp.mean(d_norm * own_normed, axis=-1, keepdims=True)
        )

        def shuffle(columns):
            def change(value):
                got = [lax.dynamic_index_in_dim(value, me, 0, False)] + [
                    swap(lax.dynamic_index_in_dim(value, me ^ j, 0, False), "shard", shards, j)
                    for j in range(1, shards)
                ]
                full = absolute(jnp.stack(got), list(range(shards)), me)
                return columns(full)

            return change

        bits = powers(reps)
        n_bits = len(bits)
        tot_down = all_reduce(g_down, [0] * n_bits, bits, mr, reps)
        alt = [bits[1], bits[0]] + bits[2:]
        tot_up = all_reduce(
            g_up.reshape(shards, rows, wide),
            [1, 1] + [1] * (n_bits - 2),
            alt,
            mr,
            reps,
            (2, shuffle(lambda v: v.transpose(1, 0, 2).reshape(v.shape[1], -1))),
        )
        tot_out = all_reduce(g_out, [1] + [0, 0] + [1] * (n_bits - 3), bits, mr, reps)
        tot_qkv = all_reduce(
            g_qkv.reshape(shards, rows, 3 * rows),
            [1, 1] + [1] * (n_bits - 2),
            bits,
            mr,
            reps,
            (
                2,
                shuffle(
                    lambda v: v.reshape(shards, v.shape[1], 3, rows)
                    .transpose(1, 2, 0, 3)
                    .reshape(v.shape[1], -1)
                ),
            ),
        )

        def by_owner(vector):
            return vector.reshape(shards, -1)

        zero_qkv = jnp.zeros((3, width), F32)
        spread = lax.dynamic_update_slice(zero_qkv, grad_bqkv.reshape(3, rows), (0, me * rows))
        vec = jnp.concatenate(
            [
                by_owner(jnp.sum(d_hid_one * normed, axis=0)),
                by_owner(jnp.sum(d_hid_one, axis=0)),
                by_owner(jnp.sum(d_hid_two * normed, axis=0)),
                by_owner(jnp.sum(d_hid_two, axis=0)),
                by_owner(spread),
            ],
            axis=1,
        )
        vec_rel = jnp.stack([lax.dynamic_index_in_dim(vec, me ^ j, 0, False) for j in order])
        mine = cube_scatter(vec_rel, "shard", shards)
        cot_sum = lax.dynamic_slice_in_dim(jnp.sum(as_float(cotan), axis=0), me * rows, rows)
        mine = jnp.concatenate([mine, cot_sum, grad_bup])
        for bit in bits:
            mine = mine + swap(mine, "rep", reps, bit)
        g1, bb1, g2, bb2 = [mine[k * rows : (k + 1) * rows] for k in range(4)]
        tot_bqkv = mine[4 * rows : 7 * rows]
        tot_cot = mine[7 * rows : 8 * rows]
        tot_bup = mine[8 * rows :]
        return (
            output[None],
            d_input[None],
            tot_qkv,
            tot_bqkv,
            tot_out,
            tot_cot,
            tot_up,
            tot_bup,
            tot_down,
            tot_cot,
            g1,
            bb1,
            g2,
            bb2,
        )

    return body


def solution(mesh):
    body = make_body(mesh.shape["shard"], mesh.shape["rep"])
    return jax.shard_map(
        body,
        mesh=mesh,
        in_specs=(
            P("rep", "shard", None),
            P("rep", "shard"),
            P("rep", None),
            P("shard", None),
            P("shard"),
            P("shard", None),
            P("shard"),
            P("shard", None),
            P("shard"),
            P("shard", None),
            P("shard"),
            P("shard"),
            P("shard"),
            P("shard"),
            P("shard"),
            P("rep", "shard", None),
        ),
        out_specs=(
            P("rep", "shard", None),
            P("rep", "shard", None),
            P("shard", None),
            P("shard"),
            P("shard", None),
            P("shard"),
            P("shard", None),
            P("shard"),
            P("shard", None),
            P("shard"),
            P("shard"),
            P("shard"),
            P("shard"),
            P("shard"),
        ),
        check_vma=False,
    )
```

```python
import math

import jax
import jax.numpy as jnp
from jax import lax
from jax.experimental import pallas as pl
from jax.experimental.pallas import tpu as pltpu
from jax.sharding import PartitionSpec as P

HEAD_DIM = 64
ROT = 16

EPSILON = 1e-05
INV_ROOT_TWO = 0.7071067811865476
INV_ROOT_TWO_PI = 0.3989422804014327


BF = jnp.bfloat16
F32 = jnp.float32
VMEM_LIMIT = 48 * 1024 * 1024


def as_float(array_in):
    return array_in.astype(F32)


def dot(left, right, dims):
    return lax.dot_general(left, right, (dims, ((), ())), preferred_element_type=F32)


def normalize(values):
    centre = values - jnp.mean(values, axis=-1, keepdims=True)
    inv_std = lax.rsqrt(jnp.mean(centre * centre, axis=-1, keepdims=True) + EPSILON)
    return (centre * inv_std, inv_std)


def gelu_parts(pre_act):
    cdf = 0.5 * (1.0 + lax.erf(pre_act * INV_ROOT_TWO))
    return pre_act * cdf, cdf + pre_act * jnp.exp(-0.5 * pre_act * pre_act) * INV_ROOT_TWO_PI


def swap(value, axis, size, bit):
    return lax.ppermute(value, axis, [(i, i ^ bit) for i in range(size)])


def powers(size):
    return [1 << k for k in range(size.bit_length() - 1)]


def cube_gather(value, axis, size):
    buf, order = value[None], [0]
    for bit in reversed(powers(size)):
        buf = jnp.concatenate([buf, swap(buf, axis, size, bit)])
        order = order + [j ^ bit for j in order]
    return buf, order


def cube_scatter(value, axis, size):
    for bit in powers(size):
        half = value.shape[0] // 2
        value = value[:half] + swap(value[half:], axis, size, bit)
    return value[0]


def absolute(blocks, order, me):
    place = {off: k for k, off in enumerate(order)}
    table = jnp.array([place[i] for i in range(len(order))], jnp.int32)
    idx = table[jnp.arange(len(order)) ^ me]
    return jnp.stack([lax.dynamic_index_in_dim(blocks, idx[i], 0, False) for i in range(len(order))])


def call(kernel, outs, ins, scratch=(), flops=0):
    shapes = [jax.ShapeDtypeStruct(s, d) for s, d in outs]
    moved = sum(math.prod(v.shape) * v.dtype.itemsize for v in [*ins, *shapes])
    return pl.pallas_call(
        kernel,
        out_shape=shapes,
        in_specs=[pl.BlockSpec(memory_space=pltpu.VMEM)] * len(ins),
        out_specs=[pl.BlockSpec(memory_space=pltpu.VMEM)] * len(shapes),
        scratch_shapes=[pltpu.VMEM(s, d) for s, d in scratch],
        compiler_params=pltpu.CompilerParams(vmem_limit_bytes=VMEM_LIMIT),
        cost_estimate=pl.CostEstimate(flops=flops, bytes_accessed=moved, transcendentals=0),
    )(*ins)


def bit_of(axis, bit):
    return jnp.where((lax.axis_index(axis) & bit) != 0, 1, 0).astype(jnp.int32)


def pack_kernel(wq, wu, q0, q1, q2, q3, u0, u1, u2, u3, scr):
    me = lax.axis_index("shard")
    rows = wq.shape[0]
    width = wq.shape[1] // 3
    wide = u0.shape[1]
    n_h = rows // HEAD_DIM
    for t in range(4):
        base = rows * t
        for h in range(n_h):
            a = base + HEAD_DIM * h
            scr[t, :, 2 * HEAD_DIM * h : 2 * HEAD_DIM * h + HEAD_DIM] = wq[:, a : a + HEAD_DIM]
            scr[t, :, 2 * HEAD_DIM * h + HEAD_DIM : 2 * HEAD_DIM * (h + 1)] = wq[
                :, width + a : width + a + HEAD_DIM
            ]
        scr[t, :, 2 * rows : 3 * rows] = wq[:, 2 * width + base : 2 * width + base + rows]
    for k, (q, u) in enumerate(((q0, u0), (q1, u1), (q2, u2), (q3, u3))):
        t = me ^ k
        q[...] = scr[t]
        u[...] = wu[:, pl.ds(pl.multiple_of(t * wide, 128), wide)]


def normed_of(ref):
    return normalize(ref[...].astype(F32))[0]


def write_rows(send, keep, grid, mine, place):
    for target, half in ((send, 1 - mine), (keep, mine)):
        n_b, n_t, n_r, _ = target.shape
        for b in range(n_b):
            for t in range(n_t):
                start = pl.multiple_of(place(half, b, t), 16)
                target[b, t] = grid[pl.ds(start, n_r), :]


def att_kernel(bit, x0, x1, x2, x3, c0, c1, c2, c3, q0, q1, q2, q3, gain, bias, bq, ca, sa, sb,
               segc, segr, idc, idr, wo,
               send, keep, att_o, dproj_o, wfull, bsum, csum, hid, cot, grid, neg):
    me = lax.axis_index("shard")
    mine = bit_of("rep", bit)
    rows, width = wo.shape
    count = x0.shape[0]
    n_h = rows // HEAD_DIM
    for j, (x, c, q) in enumerate(((x0, c0, q0), (x1, c1, q1), (x2, c2, q2), (x3, c3, q3))):
        hid[count * j : count * (j + 1), :] = (normed_of(x) * gain[...] + bias[...]).astype(BF)
        cot[count * j : count * (j + 1), :] = c[...]
        wfull[pl.ds(pl.multiple_of((me ^ j) * rows, 16), rows), :] = q[...]
    allowed = (idr[...] <= idc[...]) & (segc[...] == segr[...])
    neg[...] = jnp.where(allowed, 0.0, -jnp.inf)
    proj = dot(hid[...], wfull[...], ((1,), (0,))) + bq[...]
    d_att = dot(cot[...], wo[...], ((1,), (1,))).astype(BF)
    for h in range(n_h):
        two = 2 * HEAD_DIM
        qk = proj[:, two * h : two * (h + 1)]
        qk = qk * ca[...] + pltpu.roll(qk, two - ROT // 2, 1) * sa[...] + pltpu.roll(qk, ROT // 2, 1) * sb[...]
        qk = qk.astype(BF)
        query, key = qk[:, :HEAD_DIM], qk[:, HEAD_DIM:]
        vals = slice(2 * rows + HEAD_DIM * h, 2 * rows + HEAD_DIM * (h + 1))
        val = proj[:, vals].astype(BF)
        da = d_att[:, HEAD_DIM * h : HEAD_DIM * (h + 1)]
        scores = dot(query, key, ((1,), (1,))) * 0.125 + neg[...]
        top = jnp.max(scores, axis=-1, keepdims=True)
        expo = jnp.exp(scores - top)
        prob = expo * (1.0 / jnp.sum(expo, axis=-1, keepdims=True))
        prob_b = prob.astype(BF)
        att = dot(prob_b, val, ((1,), (0,))).astype(BF)
        att_o[:, HEAD_DIM * h : HEAD_DIM * (h + 1)] = att
        d_val = dot(prob_b, da, ((0,), (0,)))
        d_prob = dot(da, val, ((1,), (1,)))
        row_dot = jnp.sum(as_float(da) * as_float(att), axis=-1, keepdims=True)
        d_score = (prob * (d_prob - row_dot) * 0.125).astype(BF)
        dqk = jnp.concatenate(
            [dot(d_score, key, ((1,), (0,))), dot(d_score, query, ((0,), (0,)))], axis=1
        )
        dqk = dqk * ca[...] - pltpu.roll(dqk, two - ROT // 2, 1) * sa[...] - pltpu.roll(dqk, ROT // 2, 1) * sb[...]
        dproj_o[:, two * h : two * (h + 1)] = dqk.astype(BF)
        dproj_o[:, vals] = d_val.astype(BF)
        bsum[:, two * h : two * (h + 1)] = jnp.sum(dqk, axis=0, keepdims=True)
        bsum[:, vals] = jnp.sum(d_val, axis=0, keepdims=True)
    csum[...] = jnp.sum(as_float(cot[...]), axis=0, keepdims=True)
    grid[:, : 3 * rows] = dot(hid[...], dproj_o[...], ((0,), (0,))).astype(BF)
    g_out = dot(att_o[...], cot[...], ((0,), (0,))).astype(BF)
    for t in range(width // rows):
        grid[rows * t : rows * (t + 1), 3 * rows :] = g_out[:, rows * t : rows * (t + 1)]
    n_r = send.shape[2]
    write_rows(send, keep, grid, mine, lambda half, b, t: t * rows + (2 * half + b) * n_r)


def mlp1_kernel(bit, x0, x1, x2, x3, c0, c1, c2, c3, u0, u1, u2, u3, gain, bias, bup,
                send, keep, hid, activ, slope, wfull, cot, grid):
    me = lax.axis_index("shard")
    mine = bit_of("rep", bit)
    count = x0.shape[0]
    rows = u0.shape[0]
    for j, (x, c, u) in enumerate(((x0, c0, u0), (x1, c1, u1), (x2, c2, u2), (x3, c3, u3))):
        hid[count * j : count * (j + 1), :] = (normed_of(x) * gain[...] + bias[...]).astype(BF)
        cot[count * j : count * (j + 1), :] = c[...]
        wfull[pl.ds(pl.multiple_of((me ^ j) * rows, 16), rows), :] = u[...]
    for j in range(4):
        part = slice(count * j, count * (j + 1))
        pre_act = dot(hid[part, :], wfull[...], ((1,), (0,))) + bup[...]
        act, slp = gelu_parts(pre_act)
        activ[part, :] = act.astype(BF)
        slope[part, :] = slp
    grid[...] = dot(activ[...], cot[...], ((0,), (0,))).astype(BF)
    n_b, n_t, n_r, _ = send.shape
    write_rows(send, keep, grid, mine, lambda half, b, t: ((half * n_b + b) * n_t + t) * n_r)


def mlp2_kernel(bit, c0, c1, c2, c3, hid, slope, wd, send, keep, dpre, bsum, grid):
    mine = bit_of("rep", bit)
    count = c0.shape[0]
    total = None
    for j, c in enumerate((c0, c1, c2, c3)):
        part = slice(count * j, count * (j + 1))
        d_pre = dot(c[...], wd[...], ((1,), (1,))) * slope[part, :]
        dpre[part, :] = d_pre.astype(BF)
        piece = jnp.sum(d_pre, axis=0, keepdims=True)
        total = piece if total is None else total + piece
    bsum[...] = total
    grid[...] = dot(hid[...], dpre[...], ((0,), (0,))).astype(BF)
    n_b, n_t, n_r, _ = send.shape
    rows = n_r * n_b * 2
    write_rows(send, keep, grid, mine, lambda half, b, t: t * rows + (2 * half + b) * n_r)


def mlp3_kernel(x0, x1, x2, x3, att, activ, dproj, dpre, wo, wd, wq, wu, gain1, gain2,
                send, keep, sums):
    count = x0.shape[0]
    total = [None] * 4
    for j, x in enumerate((x0, x1, x2, x3)):
        part = slice(count * j, count * (j + 1))
        out = dot(att[part, :], wo[...], ((1,), (0,))) + dot(activ[part, :], wd[...], ((1,), (0,)))
        one = dot(dproj[part, :], wq[...], ((1,), (1,)))
        two = dot(dpre[part, :], wu[...], ((1,), (1,)))
        normed = normed_of(x)
        target = keep if j % 2 == 0 else send
        target[j // 2, 0] = out.astype(BF)
        target[j // 2, 1] = (one * gain1[...] + two * gain2[...]).astype(BF)
        for k, value in enumerate((one * normed, one, two * normed, two)):
            piece = jnp.sum(value, axis=0, keepdims=True)
            total[k] = piece if total[k] is None else total[k] + piece
    for k in range(4):
        sums[k : k + 1, :] = total[k]


def add_split_kernel(bit, kept, got, send, keep):
    mine = bit_of("rep", bit)
    send[...] = (as_float(kept[1 - mine]) + as_float(got[1 - mine])).astype(BF)
    keep[...] = (as_float(kept[mine]) + as_float(got[mine])).astype(BF)


def add_pieces_kernel(kept, got, p0, p1, p2, p3, *rest):
    me = lax.axis_index("shard")
    cols = p0.shape[1]
    for k, p in enumerate((p0, p1, p2, p3)):
        t = me ^ k
        total = (as_float(kept[t]) + as_float(got[t])).astype(BF)
        p[...] = total[:, :cols]
        if rest:
            rest[0][t] = total[:, cols:]


def pieces_split_kernel(bit, p0, p1, p2, p3, *rest):
    me = lax.axis_index("shard")
    mine = bit_of("rep", bit)
    send, keep = rest[-2:]
    cols = p0.shape[1]
    for k, p in enumerate((p0, p1, p2, p3)):
        s = me ^ k
        pair, slot = s >> 1, s & 1
        for target, wanted in ((keep, mine), (send, 1 - mine)):

            @pl.when(pair == wanted)
            def _(target=target):
                target[slot, :, :cols] = p[...]
                if len(rest) > 2:
                    target[slot, :, cols:] = rest[0][s]


def pair_kernel(bit, own, got, out):
    mine = bit_of("rep", bit)
    out[mine] = own[...]
    out[1 - mine] = got[...]


def final_down_kernel(bit, own, got, out):
    mine = bit_of("rep", bit)
    n_b, n_t, n_r, _ = own.shape
    for half, value in ((mine, own), (1 - mine, got)):
        for b in range(n_b):
            for t in range(n_t):
                start = pl.multiple_of(((half * n_b + b) * n_t + t) * n_r, 8)
                out[pl.ds(start, n_r), :] = as_float(value[b, t])


def final_up_kernel(bit, own, got, out):
    mine = bit_of("rep", bit)
    n_b, n_s, n_r, wide = own.shape
    for half, value in ((mine, own), (1 - mine, got)):
        for b in range(n_b):
            start = pl.multiple_of((half * n_b + b) * n_r, 8)
            for s in range(n_s):
                out[pl.ds(start, n_r), wide * s : wide * (s + 1)] = as_float(value[b, s])


def final_qkv_kernel(bit, own, got, out, out_w):
    mine = bit_of("rep", bit)
    n_b, n_s, n_r, width = own.shape
    rows = out_w.shape[0]
    n_h = rows // HEAD_DIM
    for half, value in ((mine, own), (1 - mine, got)):
        for b in range(n_b):
            place = pl.ds(pl.multiple_of((half * n_b + b) * n_r, 8), n_r)
            for s in range(n_s):
                block = as_float(value[b, s])
                for h in range(n_h):
                    a = rows * s + HEAD_DIM * h
                    two = 2 * HEAD_DIM * h
                    out[place, a : a + HEAD_DIM] = block[:, two : two + HEAD_DIM]
                    out[place, width + a : width + a + HEAD_DIM] = block[:, two + HEAD_DIM : two + 2 * HEAD_DIM]
                out[place, 2 * width + rows * s : 2 * width + rows * (s + 1)] = block[:, 2 * rows : 3 * rows]
                out_w[place, rows * s : rows * (s + 1)] = block[:, 3 * rows :]


def make_body(shards, reps):
    def body(
        block_input,
        positions,
        segments,
        w_qkv,
        b_qkv,
        w_out,
        b_out,
        w_up,
        b_up,
        w_down,
        b_down,
        ln1_gain,
        ln1_bias,
        ln2_gain,
        ln2_bias,
        cotangent,
    ):
        me = lax.axis_index("shard")
        tokens_in = block_input[0]
        cotan_own = cotangent[0]
        count, width = tokens_in.shape
        length = segments.shape[1]
        rows = w_qkv.shape[0]
        wide = w_up.shape[1] // shards
        bits = powers(reps)

        def to(j, value):
            return swap(value, "shard", shards, j)

        def gather(value):
            two = to(2, value)
            one = to(1, value)
            return value, one, two, to(1, two)

        x = gather(tokens_in)
        packed = call(
            pack_kernel,
            [((rows, 3 * rows), BF)] * 4 + [((rows, wide), BF)] * 4,
            (w_qkv, w_up),
            scratch=[((4, rows, 3 * rows), BF)],
        )
        q_w = (packed[0], to(1, packed[1]), to(2, packed[2]), to(3, packed[3]))
        c = gather(cotan_own)
        u_w = (packed[4], to(1, packed[5]), to(2, packed[6]), to(3, packed[7]))

        position = positions[0]
        small = jnp.concatenate(
            [
                ln1_gain,
                ln1_bias,
                ln2_gain,
                ln2_bias,
                b_out,
                b_down,
                b_qkv,
                (position >> 5).astype(BF),
                (position & 31).astype(BF),
            ]
        )
        small_rel, order = cube_gather(small, "shard", shards)
        small_abs = absolute(small_rel, order, me)
        cuts = [0]
        for part in (rows, rows, rows, rows, rows, rows, 3 * rows, count, count):
            cuts.append(cuts[-1] + part)
        pieces = [small_abs[:, a:b] for a, b in zip(cuts[:-1], cuts[1:])]
        gain_one, bias_one, gain_two, bias_two, full_bout, full_bdown = [
            as_float(p.reshape(1, -1)) for p in pieces[:6]
        ]
        own_b = lax.dynamic_slice_in_dim(pieces[6].reshape(3, width), me * rows, rows, 1)
        n_h = rows // HEAD_DIM
        bias_qkv = as_float(
            jnp.concatenate(
                [
                    own_b[:2].reshape(2, n_h, HEAD_DIM).transpose(1, 0, 2).reshape(-1),
                    own_b[2],
                ]
            )
        ).reshape(1, -1)
        digits = [small_rel[order.index(j)] for j in range(shards)]
        pos_rel = jnp.concatenate(
            [
                d[cuts[7] : cuts[8]].astype(jnp.int32) * 32 + d[cuts[8] : cuts[9]].astype(jnp.int32)
                for d in digits
            ]
        )
        places = jnp.concatenate(
            [(me ^ j) * count + jnp.arange(count, dtype=jnp.int32) for j in range(shards)]
        )
        seg_abs = segments[0].reshape(shards, count)
        seg_rel = jnp.concatenate(
            [lax.dynamic_index_in_dim(seg_abs, me ^ j, 0, False) for j in range(shards)]
        )
        half = ROT // 2
        lane = jnp.arange(2 * HEAD_DIM) % HEAD_DIM
        freqs = jnp.exp((lane % half).astype(F32) * (-math.log(10000.0) / half))
        angles = pos_rel.astype(F32)[:, None] * freqs[None, :]
        cosine, sine = jnp.cos(angles), jnp.sin(angles)
        ca = jnp.where(lane < ROT, cosine, 1.0)
        sa = jnp.where(lane < half, -sine, 0.0)
        sb = jnp.where((lane >= half) & (lane < ROT), sine, 0.0)

        first, second, third = bits[:3]
        order_att, order_down, order_up = (first, second), (second, first), (first, second)
        sub = rows // 4
        n_c = width // rows

        sent_c, kept_c, att, dproj, wq_full, bsum, csum = call(
            lambda *refs: att_kernel(order_att[0], *refs),
            [((2, n_c, sub, width), BF)] * 2
            + [
                ((length, rows), BF),
                ((length, 3 * rows), BF),
                ((width, 3 * rows), BF),
                ((1, 3 * rows), F32),
                ((1, width), F32),
            ],
            (*x, *c, *q_w, gain_one, bias_one, bias_qkv, ca, sa, sb,
             seg_rel[:, None], seg_rel[None, :], places[:, None], places[None, :], w_out),
            scratch=[((length, width), BF), ((length, width), BF), ((width, width), BF), ((length, length), F32)],
            flops=4_000_000_000,
        )
        sent_a, kept_a, hid_two, activ, slope, wu_full = call(
            lambda *refs: mlp1_kernel(order_down[0], *refs),
            [((2, 2, wide // 8, width), BF)] * 2
            + [((length, width), BF), ((length, wide), BF), ((length, wide), F32), ((width, wide), BF)],
            (*x, *c, *u_w, gain_two, bias_two, as_float(b_up).reshape(1, -1)),
            scratch=[((length, width), BF), ((wide, width), BF)],
            flops=2_000_000_000,
        )
        sent_b, kept_b, dpre, bup_sum = call(
            lambda *refs: mlp2_kernel(order_up[0], *refs),
            [((2, shards, sub, wide), BF)] * 2 + [((length, wide), BF), ((1, wide), F32)],
            (*c, hid_two, slope, w_down),
            scratch=[((width, wide), BF)],
            flops=2_000_000_000,
        )
        rs_send, rs_keep, ln_sums = call(
            mlp3_kernel,
            [((2, 2, count, width), BF)] * 2 + [((4, width), F32)],
            (*x, att, activ, dproj, dpre, w_out, w_down, wq_full, wu_full, gain_one, gain_two),
            flops=3_000_000_000,
        )

        def over(bit, value):
            return swap(value, "rep", reps, bit)

        def add_split(bit, kept, got):
            return call(
                lambda *refs: add_split_kernel(bit, *refs), [(kept.shape[1:], BF)] * 2, (kept, got)
            )

        def pair(bit, own):
            return call(
                lambda *refs: pair_kernel(bit, *refs), [((2, *own.shape), BF)], (own, over(bit, own))
            )[0]

        def finish_sum(kept, got):
            own = (as_float(kept) + as_float(got)).astype(BF)
            for bit in bits[3:]:
                own = (as_float(own) + as_float(over(bit, own))).astype(BF)
            return lax.optimization_barrier(own)

        def shard_stream(bit_order, sent, kept, cols):
            one, two = bit_order
            sent, kept = add_split(two, kept, over(one, sent))
            got = over(two, sent)
            extra = [] if cols == kept.shape[2] else [((n_c, sub, kept.shape[2] - cols), BF)]
            parts = call(add_pieces_kernel, [((sub, cols), BF)] * 4 + extra, (kept, got))
            mixed = (parts[0], *(to(j, parts[j]) for j in range(1, 4)), *parts[4:])
            sent, kept = call(
                lambda *refs: pieces_split_kernel(third, *refs),
                [((2, sub, kept.shape[2]), BF)] * 2,
                mixed,
            )
            own = finish_sum(kept, over(third, sent))
            own = pair(third, own).reshape(4, sub, own.shape[2])
            own = pair(two, own)
            return own, over(one, own)

        def plain_stream(bit_order, sent, kept):
            one, two = bit_order
            sent, kept = add_split(two, kept, over(one, sent))
            sent, kept = add_split(third, kept, over(two, sent))
            own = pair(third, finish_sum(kept, over(third, sent)))
            own = pair(two, own)
            return own, over(one, own)

        own_c = shard_stream(order_att, sent_c, kept_c, 3 * rows)
        own_a = plain_stream(order_down, sent_a, kept_a)
        own_b = shard_stream(order_up, sent_b, kept_b, wide)
        tot_qkv, tot_out = call(
            lambda *refs: final_qkv_kernel(order_att[0], *refs),
            [((rows, 3 * width), F32), ((rows, width), F32)],
            own_c,
        )
        (tot_down,) = call(
            lambda *refs: final_down_kernel(order_down[0], *refs), [((wide, width), F32)], own_a
        )
        (tot_up,) = call(
            lambda *refs: final_up_kernel(order_up[0], *refs), [((rows, shards * wide), F32)], own_b
        )

        total = as_float(rs_keep) + as_float(to(1, rs_send))
        total = total[0] + as_float(to(2, total[1].astype(BF)))
        output = as_float(tokens_in) + total[0] + full_bout + full_bdown
        d_norm = total[1]
        own_normed, inv_std = normalize(as_float(tokens_in))
        d_input = as_float(cotan_own) + inv_std * (
            d_norm
            - jnp.mean(d_norm, axis=-1, keepdims=True)
            - own_normed * jnp.mean(d_norm * own_normed, axis=-1, keepdims=True)
        )

        qk_sum = bsum[0, : 2 * rows].reshape(n_h, 2, HEAD_DIM).transpose(1, 0, 2).reshape(2, rows)
        grad_bqkv = jnp.concatenate([qk_sum, bsum[:, 2 * rows :]])
        spread = lax.dynamic_update_slice(jnp.zeros((3, width), F32), grad_bqkv, (0, me * rows))
        vec = jnp.concatenate(
            [ln_sums[k].reshape(shards, -1) for k in range(4)] + [spread.reshape(shards, -1)], axis=1
        )
        vec_rel = jnp.stack([lax.dynamic_index_in_dim(vec, me ^ j, 0, False) for j in order])
        mine = cube_scatter(vec_rel, "shard", shards)
        cot_sum = lax.dynamic_slice_in_dim(csum[0], me * rows, rows)
        mine = jnp.concatenate([mine, cot_sum, bup_sum[0]])
        for bit in bits:
            mine = mine + over(bit, mine)
        g1, bb1, g2, bb2 = [mine[k * rows : (k + 1) * rows] for k in range(4)]
        tot_bqkv = mine[4 * rows : 7 * rows]
        tot_cot = mine[7 * rows : 8 * rows]
        tot_bup = mine[8 * rows :]
        return (
            output[None],
            d_input[None],
            tot_qkv,
            tot_bqkv,
            tot_out,
            tot_cot,
            tot_up,
            tot_bup,
            tot_down,
            tot_cot,
            g1,
            bb1,
            g2,
            bb2,
        )

    return body


def solution(mesh):
    body = make_body(mesh.shape["shard"], mesh.shape["rep"])
    return jax.shard_map(
        body,
        mesh=mesh,
        in_specs=(
            P("rep", "shard", None),
            P("rep", "shard"),
            P("rep", None),
            P("shard", None),
            P("shard"),
            P("shard", None),
            P("shard"),
            P("shard", None),
            P("shard"),
            P("shard", None),
            P("shard"),
            P("shard"),
            P("shard"),
            P("shard"),
            P("shard"),
            P("rep", "shard", None),
        ),
        out_specs=(
            P("rep", "shard", None),
            P("rep", "shard", None),
            P("shard", None),
            P("shard"),
            P("shard", None),
            P("shard"),
            P("shard", None),
            P("shard"),
            P("shard", None),
            P("shard"),
            P("shard"),
            P("shard"),
            P("shard"),
            P("shard"),
        ),
        check_vma=False,
    )
```

```python
import math

import jax
import jax.numpy as jnp
from jax import lax
from jax.experimental import pallas as pl
from jax.experimental.pallas import tpu as pltpu
from jax.sharding import PartitionSpec as P


HEAD_DIM = 64
ROT = 16

EPSILON = 1e-05
INV_ROOT_TWO = 0.7071067811865476
INV_ROOT_TWO_PI = 0.3989422804014327


BF = jnp.bfloat16
F32 = jnp.float32


def as_float(array_in):
    return array_in.astype(F32)


def dot(left, right, dims):
    return lax.dot_general(left, right, (dims, ((), ())), preferred_element_type=F32)


def normalize(values):
    centre = values - jnp.mean(values, axis=-1, keepdims=True)
    inv_std = lax.rsqrt(jnp.mean(centre * centre, axis=-1, keepdims=True) + EPSILON)
    return (centre * inv_std, inv_std)


def gelu_parts(pre_act):
    cdf = 0.5 * (1.0 + lax.erf(pre_act * INV_ROOT_TWO))
    return pre_act * cdf, cdf + pre_act * jnp.exp(-0.5 * pre_act * pre_act) * INV_ROOT_TWO_PI


def swap(value, axis, size, bit):
    return lax.ppermute(value, axis, [(i, i ^ bit) for i in range(size)])


def powers(size):
    return [1 << k for k in range(size.bit_length() - 1)]


def cube_gather(value, axis, size):
    buf, order = value[None], [0]
    for bit in reversed(powers(size)):
        buf = jnp.concatenate([buf, swap(buf, axis, size, bit)])
        order = order + [j ^ bit for j in order]
    return buf, order


def cube_scatter(value, axis, size):
    for bit in powers(size):
        half = value.shape[0] // 2
        value = value[:half] + swap(value[half:], axis, size, bit)
    return value[0]


def absolute(blocks, order, me):
    place = {off: k for k, off in enumerate(order)}
    table = jnp.array([place[i] for i in range(len(order))], jnp.int32)
    idx = table[jnp.arange(len(order)) ^ me]
    return jnp.stack([lax.dynamic_index_in_dim(blocks, idx[i], 0, False) for i in range(len(order))])


def call(kernel, outs, ins, scratch=(), flops=0, limit=8):
    shapes = [jax.ShapeDtypeStruct(s, d) for s, d in outs]
    moved = sum(math.prod(v.shape) * v.dtype.itemsize for v in [*ins, *shapes])
    return pl.pallas_call(
        kernel,
        out_shape=shapes,
        scratch_shapes=[pltpu.VMEM(s, d) for s, d in scratch],
        compiler_params=pltpu.CompilerParams(vmem_limit_bytes=limit * 1024 * 1024),
        cost_estimate=pl.CostEstimate(flops=flops, bytes_accessed=moved, transcendentals=0),
    )(*ins)


def bit_of(axis, bit):
    return jnp.where((lax.axis_index(axis) & bit) != 0, 1, 0).astype(jnp.int32)


def pack_kernel(wq, wu, q0, q1, q2, q3, u0, u1, u2, u3, scr):
    me = lax.axis_index("shard")
    rows = wq.shape[0]
    width = wq.shape[1] // 3
    wide = u0.shape[1]
    n_h = rows // HEAD_DIM
    for t in range(4):
        base = rows * t
        for h in range(n_h):
            a = base + HEAD_DIM * h
            scr[t, :, 2 * HEAD_DIM * h : 2 * HEAD_DIM * h + HEAD_DIM] = wq[:, a : a + HEAD_DIM]
            scr[t, :, 2 * HEAD_DIM * h + HEAD_DIM : 2 * HEAD_DIM * (h + 1)] = wq[
                :, width + a : width + a + HEAD_DIM
            ]
        scr[t, :, 2 * rows : 3 * rows] = wq[:, 2 * width + base : 2 * width + base + rows]
    for k, (q, u) in enumerate(((q0, u0), (q1, u1), (q2, u2), (q3, u3))):
        t = me ^ k
        q[...] = scr[t]
        u[...] = wu[:, pl.ds(pl.multiple_of(t * wide, 128), wide)]


def normed_of(ref):
    return normalize(ref[...].astype(F32))[0]


def write_rows(targets, grid, first, second, place):
    for target, half, b in zip(
        targets, (1 - first, 1 - first, first, first), (1 - second, second, 1 - second, second)
    ):
        n_t, n_r, _ = target.shape
        for t in range(n_t):
            start = pl.multiple_of(place(half, b, t), 16)
            target[t] = grid[pl.ds(start, n_r), :]


def att_kernel(order, x0, x1, x2, x3, c0, c1, c2, c3, q0, q1, q2, q3, gain, bias, bq, ca, sa, sb,
               segc, segr, idc, idr, wo,
               sa_o, sb_o, ka_o, kb_o, att_o, dproj_o, wfull, bsum, csum, hid, cot, grid, neg):
    me = lax.axis_index("shard")
    first, second = (bit_of("rep", bit) for bit in order)
    rows, width = wo.shape
    count = x0.shape[0]
    n_h = rows // HEAD_DIM
    for j, (x, c, q) in enumerate(((x0, c0, q0), (x1, c1, q1), (x2, c2, q2), (x3, c3, q3))):
        hid[count * j : count * (j + 1), :] = (normed_of(x) * gain[...] + bias[...]).astype(BF)
        cot[count * j : count * (j + 1), :] = c[...]
        wfull[pl.ds(pl.multiple_of((me ^ j) * rows, 16), rows), :] = q[...]
    allowed = (idr[...] <= idc[...]) & (segc[...] == segr[...])
    neg[...] = jnp.where(allowed, 0.0, -jnp.inf)
    proj = dot(hid[...], wfull[...], ((1,), (0,))) + bq[...]
    d_att = dot(cot[...], wo[...], ((1,), (1,))).astype(BF)
    for h in range(n_h):
        two = 2 * HEAD_DIM
        qk = proj[:, two * h : two * (h + 1)]
        qk = qk * ca[...] + pltpu.roll(qk, two - ROT // 2, 1) * sa[...] + pltpu.roll(qk, ROT // 2, 1) * sb[...]
        qk = qk.astype(BF)
        query, key = qk[:, :HEAD_DIM], qk[:, HEAD_DIM:]
        vals = slice(2 * rows + HEAD_DIM * h, 2 * rows + HEAD_DIM * (h + 1))
        val = proj[:, vals].astype(BF)
        da = d_att[:, HEAD_DIM * h : HEAD_DIM * (h + 1)]
        scores = dot(query, key, ((1,), (1,))) * 0.125 + neg[...]
        top = jnp.max(scores, axis=-1, keepdims=True)
        expo = jnp.exp(scores - top)
        prob = expo * (1.0 / jnp.sum(expo, axis=-1, keepdims=True))
        prob_b = prob.astype(BF)
        att = dot(prob_b, val, ((1,), (0,))).astype(BF)
        att_o[:, HEAD_DIM * h : HEAD_DIM * (h + 1)] = att
        d_val = dot(prob_b, da, ((0,), (0,)))
        d_prob = dot(da, val, ((1,), (1,)))
        row_dot = jnp.sum(as_float(da) * as_float(att), axis=-1, keepdims=True)
        d_score = (prob * (d_prob - row_dot) * 0.125).astype(BF)
        dqk = jnp.concatenate(
            [dot(d_score, key, ((1,), (0,))), dot(d_score, query, ((0,), (0,)))], axis=1
        )
        dqk = dqk * ca[...] - pltpu.roll(dqk, two - ROT // 2, 1) * sa[...] - pltpu.roll(dqk, ROT // 2, 1) * sb[...]
        dproj_o[:, two * h : two * (h + 1)] = dqk.astype(BF)
        dproj_o[:, vals] = d_val.astype(BF)
        bsum[:, two * h : two * (h + 1)] = jnp.sum(dqk, axis=0, keepdims=True)
        bsum[:, vals] = jnp.sum(d_val, axis=0, keepdims=True)
    csum[...] = jnp.sum(as_float(cot[...]), axis=0, keepdims=True)
    grid[:, : 3 * rows] = dot(hid[...], dproj_o[...], ((0,), (0,))).astype(BF)
    g_out = dot(att_o[...], cot[...], ((0,), (0,))).astype(BF)
    for t in range(width // rows):
        grid[rows * t : rows * (t + 1), 3 * rows :] = g_out[:, rows * t : rows * (t + 1)]
    n_r = sa_o.shape[1]
    write_rows(
        (sa_o, sb_o, ka_o, kb_o), grid, first, second, lambda half, b, t: t * rows + (2 * half + b) * n_r
    )


def mlp1_kernel(order, x0, x1, x2, x3, c0, c1, c2, c3, u0, u1, u2, u3, gain, bias, bup,
                sa_o, sb_o, ka_o, kb_o, hid, activ, slope, wfull, cot, grid):
    me = lax.axis_index("shard")
    first, second = (bit_of("rep", bit) for bit in order)
    count = x0.shape[0]
    rows = u0.shape[0]
    for j, (x, c, u) in enumerate(((x0, c0, u0), (x1, c1, u1), (x2, c2, u2), (x3, c3, u3))):
        hid[count * j : count * (j + 1), :] = (normed_of(x) * gain[...] + bias[...]).astype(BF)
        cot[count * j : count * (j + 1), :] = c[...]
        wfull[pl.ds(pl.multiple_of((me ^ j) * rows, 16), rows), :] = u[...]
    for j in range(4):
        part = slice(count * j, count * (j + 1))
        pre_act = dot(hid[part, :], wfull[...], ((1,), (0,))) + bup[...]
        act, slp = gelu_parts(pre_act)
        activ[part, :] = act.astype(BF)
        slope[part, :] = slp
    grid[...] = dot(activ[...], cot[...], ((0,), (0,))).astype(BF)
    n_t, n_r, _ = sa_o.shape
    write_rows(
        (sa_o, sb_o, ka_o, kb_o), grid, first, second, lambda half, b, t: ((half * 2 + b) * n_t + t) * n_r
    )


def mlp2_kernel(order, c0, c1, c2, c3, hid, slope, wd, sa_o, sb_o, ka_o, kb_o, dpre, bsum, grid):
    first, second = (bit_of("rep", bit) for bit in order)
    count = c0.shape[0]
    total = None
    for j, c in enumerate((c0, c1, c2, c3)):
        part = slice(count * j, count * (j + 1))
        d_pre = dot(c[...], wd[...], ((1,), (1,))) * slope[part, :]
        dpre[part, :] = d_pre.astype(BF)
        piece = jnp.sum(d_pre, axis=0, keepdims=True)
        total = piece if total is None else total + piece
    bsum[...] = total
    grid[...] = dot(hid[...], dpre[...], ((0,), (0,))).astype(BF)
    n_r = sa_o.shape[1]
    rows = n_r * 4
    write_rows(
        (sa_o, sb_o, ka_o, kb_o), grid, first, second, lambda half, b, t: t * rows + (2 * half + b) * n_r
    )


def mlp3_kernel(x0, x1, x2, x3, att, activ, dproj, dpre, wo, wd, wq, wu, gain1, gain2,
                send, keep, sums):
    count = x0.shape[0]
    total = [None] * 4
    for j, x in enumerate((x0, x1, x2, x3)):
        part = slice(count * j, count * (j + 1))
        out = dot(att[part, :], wo[...], ((1,), (0,))) + dot(activ[part, :], wd[...], ((1,), (0,)))
        one = dot(dproj[part, :], wq[...], ((1,), (1,)))
        two = dot(dpre[part, :], wu[...], ((1,), (1,)))
        normed = normed_of(x)
        target = keep if j % 2 == 0 else send
        target[j // 2, 0] = out.astype(BF)
        target[j // 2, 1] = (one * gain1[...] + two * gain2[...]).astype(BF)
        for k, value in enumerate((one * normed, one, two * normed, two)):
            piece = jnp.sum(value, axis=0, keepdims=True)
            total[k] = piece if total[k] is None else total[k] + piece
    for k in range(4):
        sums[k : k + 1, :] = total[k]


def add_kernel(kept, got, out):
    out[...] = (as_float(kept[...]) + as_float(got[...])).astype(out.dtype)


def add_split_kernel(bit, kept, got, more, send, keep):
    mine = bit_of("rep", bit)
    for place, out in ((1 - mine, send), (mine, keep)):
        out[...] = (as_float(kept[place]) + as_float(got[place]) + as_float(more[place])).astype(BF)


def add_pieces_kernel(kept, got, more, p0, p1, p2, p3, *rest):
    me = lax.axis_index("shard")
    cols = p0.shape[1]
    for k, p in enumerate((p0, p1, p2, p3)):
        t = me ^ k
        total = (as_float(kept[t]) + as_float(got[t]) + as_float(more[t])).astype(BF)
        p[...] = total[:, :cols]
        if rest:
            rest[0][t] = total[:, cols:]


def pieces_split_kernel(bit, p0, p1, p2, p3, *rest):
    me = lax.axis_index("shard")
    mine = bit_of("rep", bit)
    send, keep = rest[-2:]
    cols = p0.shape[1]
    for k, p in enumerate((p0, p1, p2, p3)):
        s = me ^ k
        pair, slot = s >> 1, s & 1
        for target, wanted in ((keep, mine), (send, 1 - mine)):

            @pl.when(pair == wanted)
            def _(target=target):
                target[slot, :, :cols] = p[...]
                if len(rest) > 2:
                    target[slot, :, cols:] = rest[0][s]


def pair_kernel(bit, own, got, out):
    mine = bit_of("rep", bit)
    out[mine] = own[...]
    out[1 - mine] = got[...]


def quarters(order, refs):
    first, second = (bit_of("rep", bit) for bit in order)
    return zip(refs, (first, first, 1 - first, 1 - first), (second, 1 - second, second, 1 - second))


def final_down_kernel(order, p0, p1, p2, p3, out):
    for value, half, b in quarters(order, (p0, p1, p2, p3)):
        n_t, n_r, _ = value.shape
        for t in range(n_t):
            start = pl.multiple_of(((half * 2 + b) * n_t + t) * n_r, 8)
            out[pl.ds(start, n_r), :] = as_float(value[t])


def final_up_kernel(order, p0, p1, p2, p3, out):
    for value, half, b in quarters(order, (p0, p1, p2, p3)):
        n_s, n_r, wide = value.shape
        start = pl.multiple_of((half * 2 + b) * n_r, 8)
        for s in range(n_s):
            out[pl.ds(start, n_r), wide * s : wide * (s + 1)] = as_float(value[s])


def final_qkv_kernel(order, p0, p1, p2, p3, out, out_w):
    rows = out_w.shape[0]
    n_h = rows // HEAD_DIM
    for value, half, b in quarters(order, (p0, p1, p2, p3)):
        n_s, n_r, width = value.shape
        place = pl.ds(pl.multiple_of((half * 2 + b) * n_r, 8), n_r)
        for s in range(n_s):
            block = as_float(value[s])
            for h in range(n_h):
                a = rows * s + HEAD_DIM * h
                two = 2 * HEAD_DIM * h
                out[place, a : a + HEAD_DIM] = block[:, two : two + HEAD_DIM]
                out[place, width + a : width + a + HEAD_DIM] = block[:, two + HEAD_DIM : two + 2 * HEAD_DIM]
            out[place, 2 * width + rows * s : 2 * width + rows * (s + 1)] = block[:, 2 * rows : 3 * rows]
            out_w[place, rows * s : rows * (s + 1)] = block[:, 3 * rows :]


def make_body(shards, reps):
    def body(
        block_input,
        positions,
        segments,
        w_qkv,
        b_qkv,
        w_out,
        b_out,
        w_up,
        b_up,
        w_down,
        b_down,
        ln1_gain,
        ln1_bias,
        ln2_gain,
        ln2_bias,
        cotangent,
    ):
        me = lax.axis_index("shard")
        tokens_in = block_input[0]
        cotan_own = cotangent[0]
        count, width = tokens_in.shape
        length = segments.shape[1]
        rows = w_qkv.shape[0]
        wide = w_up.shape[1] // shards
        bits = powers(reps)

        def to(j, value):
            return swap(value, "shard", shards, j)

        def gather(value):
            two = to(2, value)
            one = to(1, value)
            return value, one, two, swap(two, "shard", shards, 1)

        x = gather(tokens_in)
        packed = call(
            pack_kernel,
            [((rows, 3 * rows), BF)] * 4 + [((rows, wide), BF)] * 4,
            (w_qkv, w_up),
            scratch=[((4, rows, 3 * rows), BF)],
        )
        q_w = (packed[0], *(to(j, packed[j]) for j in (1, 2, 3)))
        c = gather(cotan_own)
        u_w = (packed[4], *(to(j, packed[4 + j]) for j in (1, 2, 3)))

        position = positions[0]
        small = jnp.concatenate(
            [
                ln1_gain,
                ln1_bias,
                ln2_gain,
                ln2_bias,
                b_out,
                b_down,
                b_qkv,
                (position >> 5).astype(BF),
                (position & 31).astype(BF),
            ]
        )
        small_rel, order = cube_gather(small, "shard", shards)
        small_abs = absolute(small_rel, order, me)
        cuts = [0]
        for part in (rows, rows, rows, rows, rows, rows, 3 * rows, count, count):
            cuts.append(cuts[-1] + part)
        pieces = [small_abs[:, a:b] for a, b in zip(cuts[:-1], cuts[1:])]
        gain_one, bias_one, gain_two, bias_two, full_bout, full_bdown = [
            as_float(p.reshape(1, -1)) for p in pieces[:6]
        ]
        own_b = lax.dynamic_slice_in_dim(pieces[6].reshape(3, width), me * rows, rows, 1)
        n_h = rows // HEAD_DIM
        bias_qkv = as_float(
            jnp.concatenate(
                [
                    own_b[:2].reshape(2, n_h, HEAD_DIM).transpose(1, 0, 2).reshape(-1),
                    own_b[2],
                ]
            )
        ).reshape(1, -1)
        digits = [small_rel[order.index(j)] for j in range(shards)]
        pos_rel = jnp.concatenate(
            [
                d[cuts[7] : cuts[8]].astype(jnp.int32) * 32 + d[cuts[8] : cuts[9]].astype(jnp.int32)
                for d in digits
            ]
        )
        places = jnp.concatenate(
            [(me ^ j) * count + jnp.arange(count, dtype=jnp.int32) for j in range(shards)]
        )
        seg_abs = segments[0].reshape(shards, count)
        seg_rel = jnp.concatenate(
            [lax.dynamic_index_in_dim(seg_abs, me ^ j, 0, False) for j in range(shards)]
        )
        half = ROT // 2
        lane = jnp.arange(2 * HEAD_DIM) % HEAD_DIM
        freqs = jnp.exp((lane % half).astype(F32) * (-math.log(10000.0) / half))
        angles = pos_rel.astype(F32)[:, None] * freqs[None, :]
        cosine, sine = jnp.cos(angles), jnp.sin(angles)
        ca = jnp.where(lane < ROT, cosine, 1.0)
        sa = jnp.where(lane < half, -sine, 0.0)
        sb = jnp.where((lane >= half) & (lane < ROT), sine, 0.0)

        first, second, third = bits[:3]
        order_att, order_down, order_up = (first, second), (first, second), (second, first)
        sub = rows // 4
        n_c = width // rows

        *grad_a, hid_two, activ, slope, wu_full = call(
            lambda *refs: mlp1_kernel(order_down, *refs),
            [((2, wide // 8, width), BF)] * 4
            + [((length, width), BF), ((length, wide), BF), ((length, wide), F32), ((width, wide), BF)],
            (*x, *c, *u_w, gain_two, bias_two, as_float(b_up).reshape(1, -1)),
            scratch=[((length, width), BF), ((wide, width), BF)],
            flops=2_000_000_000,
            limit=24,
        )
        *grad_b, dpre, bup_sum = call(
            lambda *refs: mlp2_kernel(order_up, *refs),
            [((shards, sub, wide), BF)] * 4 + [((length, wide), BF), ((1, wide), F32)],
            (*c, hid_two, slope, w_down),
            scratch=[((width, wide), BF)],
            flops=2_000_000_000,
            limit=24,
        )
        *grad_c, att, dproj, wq_full, bsum, csum = call(
            lambda *refs: att_kernel(order_att, *refs),
            [((n_c, sub, width), BF)] * 4
            + [
                ((length, rows), BF),
                ((length, 3 * rows), BF),
                ((width, 3 * rows), BF),
                ((1, 3 * rows), F32),
                ((1, width), F32),
            ],
            (*x, *c, *q_w, gain_one, bias_one, bias_qkv, ca, sa, sb,
             seg_rel[:, None], seg_rel[None, :], places[:, None], places[None, :], w_out),
            scratch=[((length, width), BF), ((length, width), BF), ((width, width), BF), ((length, length), F32)],
            flops=4_000_000_000,
            limit=24,
        )
        rs_send, rs_keep, ln_sums = call(
            mlp3_kernel,
            [((2, 2, count, width), BF)] * 2 + [((4, width), F32)],
            (*x, att, activ, dproj, dpre, w_out, w_down, wq_full, wu_full, gain_one, gain_two),
            flops=3_000_000_000,
            limit=24,
        )

        def over(bit, value):
            return swap(value, "rep", reps, bit)

        def start_sum(bit_order, grad):
            sent_a, sent_b, kept_a, kept_b = grad
            one, two = bit_order
            got_a = over(one, sent_a)
            got_b = over(one, sent_b)
            (sent,) = call(add_kernel, [(kept_a.shape, BF)], (kept_a, got_a))
            return kept_b, got_b, over(two, sent)

        def finish_sum(bit_order, sent, kept, shape):
            one, two = bit_order
            got = over(third, sent)
            (own,) = call(add_kernel, [(kept.shape, BF)], (kept, got))
            for bit in bits[3:]:
                more = over(bit, own)
                (own,) = call(add_kernel, [(own.shape, BF)], (own, more))
            (both,) = call(lambda *refs: pair_kernel(third, *refs), [((2, *own.shape), BF)], (own, over(third, own)))
            both = both.reshape(shape)
            other = over(two, both)
            return both, other, over(one, both), over(one, other)

        def shard_stream(bit_order, grad, cols):
            held = start_sum(bit_order, grad)
            shape = held[0].shape
            extra = [] if cols == shape[2] else [((n_c, sub, shape[2] - cols), BF)]
            parts = call(add_pieces_kernel, [((sub, cols), BF)] * 4 + extra, held)
            mixed = (parts[0], *(to(j, parts[j]) for j in range(1, 4)), *parts[4:])
            sent, kept = call(lambda *refs: pieces_split_kernel(third, *refs), [((2, sub, shape[2]), BF)] * 2, mixed)
            return finish_sum(bit_order, sent, kept, shape)

        def plain_stream(bit_order, grad):
            held = start_sum(bit_order, grad)
            shape = held[0].shape
            sent, kept = call(lambda *refs: add_split_kernel(third, *refs), [(shape[1:], BF)] * 2, held)
            return finish_sum(bit_order, sent, kept, shape)

        own_c = shard_stream(order_att, grad_c, 3 * rows)
        own_a = plain_stream(order_down, grad_a)
        own_b = shard_stream(order_up, grad_b, wide)
        tot_qkv, tot_out = call(
            lambda *refs: final_qkv_kernel(order_att, *refs), [((rows, 3 * width), F32), ((rows, width), F32)], own_c
        )
        (tot_down,) = call(lambda *refs: final_down_kernel(order_down, *refs), [((wide, width), F32)], own_a)
        (tot_up,) = call(lambda *refs: final_up_kernel(order_up, *refs), [((rows, shards * wide), F32)], own_b)

        got = to(1, rs_send)
        (onward,) = call(add_kernel, [(got.shape[1:], BF)], (rs_keep[1], got[1]))
        total = as_float(rs_keep[0]) + as_float(got[0]) + as_float(to(2, onward))
        output = as_float(tokens_in) + total[0] + full_bout + full_bdown
        d_norm = total[1]
        own_normed, inv_std = normalize(as_float(tokens_in))
        d_input = as_float(cotan_own) + inv_std * (
            d_norm
            - jnp.mean(d_norm, axis=-1, keepdims=True)
            - own_normed * jnp.mean(d_norm * own_normed, axis=-1, keepdims=True)
        )

        qk_sum = bsum[0, : 2 * rows].reshape(n_h, 2, HEAD_DIM).transpose(1, 0, 2).reshape(2, rows)
        grad_bqkv = jnp.concatenate([qk_sum, bsum[:, 2 * rows :]])
        spread = lax.dynamic_update_slice(jnp.zeros((3, width), F32), grad_bqkv, (0, me * rows))
        vec = jnp.concatenate(
            [ln_sums[k].reshape(shards, -1) for k in range(4)] + [spread.reshape(shards, -1)], axis=1
        )
        vec_rel = jnp.stack([lax.dynamic_index_in_dim(vec, me ^ j, 0, False) for j in order])
        mine = cube_scatter(vec_rel, "shard", shards)
        cot_sum = lax.dynamic_slice_in_dim(csum[0], me * rows, rows)
        mine = jnp.concatenate([mine, cot_sum, bup_sum[0]])
        mine = mine.reshape(1, -1)
        for bit in bits:
            (mine,) = call(add_kernel, [(mine.shape, F32)], (mine, over(bit, mine)), limit=1)
        mine = mine.reshape(-1)
        g1, bb1, g2, bb2 = [mine[k * rows : (k + 1) * rows] for k in range(4)]
        tot_bqkv = mine[4 * rows : 7 * rows]
        tot_cot = mine[7 * rows : 8 * rows]
        tot_bup = mine[8 * rows :]
        return (
            output[None],
            d_input[None],
            tot_qkv,
            tot_bqkv,
            tot_out,
            tot_cot,
            tot_up,
            tot_bup,
            tot_down,
            tot_cot,
            g1,
            bb1,
            g2,
            bb2,
        )

    return body


def solution(mesh):
    body = make_body(mesh.shape["shard"], mesh.shape["rep"])
    return jax.shard_map(
        body,
        mesh=mesh,
        in_specs=(
            P("rep", "shard", None),
            P("rep", "shard"),
            P("rep", None),
            P("shard", None),
            P("shard"),
            P("shard", None),
            P("shard"),
            P("shard", None),
            P("shard"),
            P("shard", None),
            P("shard"),
            P("shard"),
            P("shard"),
            P("shard"),
            P("shard"),
            P("rep", "shard", None),
        ),
        out_specs=(
            P("rep", "shard", None),
            P("rep", "shard", None),
            P("shard", None),
            P("shard"),
            P("shard", None),
            P("shard"),
            P("shard", None),
            P("shard"),
            P("shard", None),
            P("shard"),
            P("shard"),
            P("shard"),
            P("shard"),
            P("shard"),
        ),
        check_vma=False,
    )
```

```python
import math

import jax
import jax.numpy as jnp
from jax import lax
from jax.experimental import pallas as pl
from jax.experimental.pallas import tpu as pltpu
from jax.sharding import PartitionSpec as P


HEAD_DIM = 64
ROT = 16

EPSILON = 1e-05
INV_ROOT_TWO = 0.7071067811865476
INV_ROOT_TWO_PI = 0.3989422804014327


BF = jnp.bfloat16
F32 = jnp.float32


def as_float(array_in):
    return array_in.astype(F32)


def dot(left, right, dims):
    return lax.dot_general(left, right, (dims, ((), ())), preferred_element_type=F32)


def normalize(values):
    centre = values - jnp.mean(values, axis=-1, keepdims=True)
    inv_std = lax.rsqrt(jnp.mean(centre * centre, axis=-1, keepdims=True) + EPSILON)
    return (centre * inv_std, inv_std)


def gelu_parts(pre_act):
    cdf = 0.5 * (1.0 + lax.erf(pre_act * INV_ROOT_TWO))
    return pre_act * cdf, cdf + pre_act * jnp.exp(-0.5 * pre_act * pre_act) * INV_ROOT_TWO_PI


def swap(value, axis, size, bit):
    return lax.ppermute(value, axis, [(i, i ^ bit) for i in range(size)])


def powers(size):
    return [1 << k for k in range(size.bit_length() - 1)]


def call(kernel, outs, ins, scratch=(), flops=0, limit=8):
    shapes = [jax.ShapeDtypeStruct(s, d) for s, d in outs]
    moved = sum(math.prod(v.shape) * v.dtype.itemsize for v in [*ins, *shapes])
    return pl.pallas_call(
        kernel,
        out_shape=shapes,
        scratch_shapes=[pltpu.VMEM(s, d) for s, d in scratch],
        compiler_params=pltpu.CompilerParams(vmem_limit_bytes=limit * 1024 * 1024),
        cost_estimate=pl.CostEstimate(flops=flops, bytes_accessed=moved, transcendentals=0),
    )(*ins)


def bit_of(axis, bit):
    return jnp.where((lax.axis_index(axis) & bit) != 0, 1, 0).astype(jnp.int32)


def pack_kernel(wq, wu, pos, g1, b1, g2, b2, bo, bd, bq, q0, q1, q2, q3, u0, u1, u2, u3, small, scr):
    me = lax.axis_index("shard")
    rows = wq.shape[0]
    count = pos.shape[1]
    for k, ref in enumerate((g1, b1, g2, b2, bo, bd)):
        small[k : k + 1, :rows] = as_float(ref[...]).reshape(1, rows)
    small[6:7, : 3 * rows] = as_float(bq[...]).reshape(1, 3 * rows)
    small[7:8, :count] = as_float(pos[...])
    width = wq.shape[1] // 3
    wide = u0.shape[1]
    n_h = rows // HEAD_DIM
    for t in range(4):
        base = rows * t
        for h in range(n_h):
            a = base + HEAD_DIM * h
            scr[t, :, 2 * HEAD_DIM * h : 2 * HEAD_DIM * h + HEAD_DIM] = wq[:, a : a + HEAD_DIM]
            scr[t, :, 2 * HEAD_DIM * h + HEAD_DIM : 2 * HEAD_DIM * (h + 1)] = wq[
                :, width + a : width + a + HEAD_DIM
            ]
        scr[t, :, 2 * rows : 3 * rows] = wq[:, 2 * width + base : 2 * width + base + rows]
    for k, (q, u) in enumerate(((q0, u0), (q1, u1), (q2, u2), (q3, u3))):
        t = me ^ k
        q[...] = scr[t]
        u[...] = wu[:, pl.ds(pl.multiple_of(t * wide, 128), wide)]


def normed_of(ref):
    return normalize(ref[...].astype(F32))[0]


def write_rows(targets, grid, first, second, place):
    for target, half, b in zip(
        targets, (1 - first, 1 - first, first, first), (1 - second, second, 1 - second, second)
    ):
        n_t, n_r, _ = target.shape
        for t in range(n_t):
            start = pl.multiple_of(place(half, b, t), 16)
            target[t] = grid[pl.ds(start, n_r), :]


def prep_kernel(x0, x1, x2, x3, c0, c1, c2, c3, s0, s1, s2, s3, wd, wo,
                hid1, hid1_t, hid2, hid2_t, cot, dact, datt, csum, vec, bq_own, pos, sm, bq):
    me = lax.axis_index("shard")
    count = x0.shape[0]
    rows = wo.shape[0]
    width = wo.shape[1]
    for j, ref in enumerate((s0, s1, s2, s3)):
        sm[me ^ j] = ref[...]
    vec[...] = jnp.zeros_like(vec)
    for s in range(4):
        for k in range(6):
            vec[k : k + 1, rows * s : rows * (s + 1)] = sm[s, k : k + 1, :rows]
        bq[:, 3 * rows * s : 3 * rows * (s + 1)] = sm[s, 6:7, :]
        pos[:, count * s : count * (s + 1)] = sm[s, 7:8, :count]
    for t in range(4):

        @pl.when(me == t)
        def _(t=t):
            for part in range(3):
                for h in range(rows // HEAD_DIM):
                    a = part * width + rows * t + HEAD_DIM * h
                    b = HEAD_DIM * (2 * h + part) if part < 2 else 2 * rows + HEAD_DIM * h
                    bq_own[:, b : b + HEAD_DIM] = bq[:, a : a + HEAD_DIM]

    gain1, bias1, gain2, bias2 = (vec[k : k + 1, :] for k in range(4))
    for j, (x, c) in enumerate(((x0, c0), (x1, c1), (x2, c2), (x3, c3))):
        place = pl.ds(pl.multiple_of((me ^ j) * count, count), count)
        normed = normed_of(x)
        hid1[place, :] = (normed * gain1 + bias1).astype(BF)
        hid2[place, :] = (normed * gain2 + bias2).astype(BF)
        cot[place, :] = c[...]
    hid1_t[...] = hid1[...].T
    hid2_t[...] = hid2[...].T
    dact[...] = dot(cot[...], wd[...], ((1,), (1,)))
    datt[...] = dot(cot[...], wo[...], ((1,), (1,))).astype(BF)
    csum[...] = jnp.sum(as_float(cot[...]), axis=0, keepdims=True)


def att_kernel(order, hid, hid_t, cot, datt, q0, q1, q2, q3, bq, ca, sa, sb, segc, segr,
               sa_o, sb_o, ka_o, kb_o, att_o, dproj_o, wfull, bsum, neg, grid):
    me = lax.axis_index("shard")
    first, second = (bit_of("rep", bit) for bit in order)
    rows = q0.shape[0]
    length, width = cot.shape
    two = 2 * HEAD_DIM
    n_h = rows // HEAD_DIM
    for j, q in enumerate((q0, q1, q2, q3)):
        wfull[pl.ds(pl.multiple_of((me ^ j) * rows, 16), rows), :] = q[...]
    col = lax.broadcasted_iota(jnp.int32, (length, length), 1)
    row = lax.broadcasted_iota(jnp.int32, (length, length), 0)
    neg[...] = jnp.where((col <= row) & (segc[...] == segr[...]), 0.0, -jnp.inf)
    proj = dot(hid[...], wfull[...], ((1,), (0,))) + bq[...]
    for h in range(n_h):
        qk = proj[:, two * h : two * (h + 1)]
        qk = qk * ca[...] + pltpu.roll(qk, two - ROT // 2, 1) * sa[...] + pltpu.roll(qk, ROT // 2, 1) * sb[...]
        qk = qk.astype(BF)
        query, key = qk[:, :HEAD_DIM], qk[:, HEAD_DIM:]
        vals = slice(2 * rows + HEAD_DIM * h, 2 * rows + HEAD_DIM * (h + 1))
        val = proj[:, vals].astype(BF)
        da = datt[:, HEAD_DIM * h : HEAD_DIM * (h + 1)]
        scores = dot(query * jnp.asarray(0.125, BF), key, ((1,), (1,))) + neg[...]
        top = jnp.max(scores, axis=-1, keepdims=True)
        expo = jnp.exp(scores - top)
        prob = expo * (1.0 / jnp.sum(expo, axis=-1, keepdims=True))
        prob_b = prob.astype(BF)
        att = dot(prob_b, val, ((1,), (0,))).astype(BF)
        att_o[:, HEAD_DIM * h : HEAD_DIM * (h + 1)] = att
        d_val = dot(prob_b, da, ((0,), (0,)))
        d_prob = dot(da, val, ((1,), (1,)))
        row_dot = jnp.sum(as_float(da) * as_float(att), axis=-1, keepdims=True)
        d_score = (prob * (d_prob - row_dot)).astype(BF)
        dqk = 0.125 * jnp.concatenate(
            [dot(d_score, key, ((1,), (0,))), dot(d_score, query, ((0,), (0,)))], axis=1
        )
        dqk = dqk * ca[...] - pltpu.roll(dqk, two - ROT // 2, 1) * sa[...] - pltpu.roll(dqk, ROT // 2, 1) * sb[...]
        dproj_o[:, two * h : two * (h + 1)] = dqk.astype(BF)
        dproj_o[:, vals] = d_val.astype(BF)
        bsum[:, two * h : two * (h + 1)] = jnp.sum(dqk, axis=0, keepdims=True)
        bsum[:, vals] = jnp.sum(d_val, axis=0, keepdims=True)
    grid[:, : 3 * rows] = dot(hid_t[...], dproj_o[...], ((1,), (0,))).astype(BF)
    g_out = dot(att_o[...], cot[...], ((0,), (0,))).astype(BF)
    for t in range(width // rows):
        grid[rows * t : rows * (t + 1), 3 * rows :] = g_out[:, rows * t : rows * (t + 1)]
    n_r = sa_o.shape[1]
    write_rows(
        (sa_o, sb_o, ka_o, kb_o), grid, first, second, lambda half, b, t: t * rows + (2 * half + b) * n_r
    )


def mlp1_kernel(order, hid, cot, u0, u1, u2, u3, bup, sa_o, sb_o, ka_o, kb_o, activ, slope, wfull, grid):
    me = lax.axis_index("shard")
    first, second = (bit_of("rep", bit) for bit in order)
    rows = u0.shape[0]
    for j, u in enumerate((u0, u1, u2, u3)):
        wfull[pl.ds(pl.multiple_of((me ^ j) * rows, 16), rows), :] = u[...]
    block = hid.shape[0] // 4
    for j in range(4):
        part = slice(block * j, block * (j + 1))
        pre_act = dot(hid[part, :], wfull[...], ((1,), (0,))) + bup[...]
        act, slp = gelu_parts(pre_act)
        activ[part, :] = act.astype(BF)
        slope[part, :] = slp
    grid[...] = dot(activ[...], cot[...], ((0,), (0,))).astype(BF)
    n_t, n_r, _ = sa_o.shape
    write_rows(
        (sa_o, sb_o, ka_o, kb_o), grid, first, second, lambda half, b, t: ((half * 2 + b) * n_t + t) * n_r
    )


def mlp2_kernel(order, dact, hid_t, slope, sa_o, sb_o, ka_o, kb_o, dpre, bsum, grid):
    first, second = (bit_of("rep", bit) for bit in order)
    d_pre = dact[...] * slope[...]
    dpre[...] = d_pre.astype(BF)
    bsum[...] = jnp.sum(d_pre, axis=0, keepdims=True)
    grid[...] = dot(hid_t[...], dpre[...], ((1,), (0,))).astype(BF)
    n_r = sa_o.shape[1]
    rows = n_r * 4
    write_rows(
        (sa_o, sb_o, ka_o, kb_o), grid, first, second, lambda half, b, t: t * rows + (2 * half + b) * n_r
    )


def mlp3_kernel(x0, x1, x2, x3, att, activ, dproj, dpre, wo, wd, wq, wu, vec,
                bsum, csum, bup, send, keep, vecs):
    me = lax.axis_index("shard")
    count = x0.shape[0]
    total = [None] * 4
    for j, x in enumerate((x0, x1, x2, x3)):
        part = pl.ds(pl.multiple_of((me ^ j) * count, count), count)
        out = dot(att[part, :], wo[...], ((1,), (0,))) + dot(activ[part, :], wd[...], ((1,), (0,)))
        one = dot(dproj[part, :], wq[...], ((1,), (1,)))
        two = dot(dpre[part, :], wu[...], ((1,), (1,)))
        normed = normed_of(x)
        target = keep if j % 2 == 0 else send
        target[j // 2, :count, :] = out.astype(BF)
        target[j // 2, count : 2 * count, :] = (one * vec[0:1, :] + two * vec[2:3, :]).astype(BF)
        for k, value in enumerate((one * normed, one, two * normed, two)):
            piece = jnp.sum(value, axis=0, keepdims=True)
            total[k] = piece if total[k] is None else total[k] + piece
    rows, _ = wo.shape
    n_h = rows // HEAD_DIM
    vecs[...] = jnp.zeros_like(vecs)
    for t in range(4):
        for k in range(4):
            vecs[t, 0:1, rows * k : rows * (k + 1)] = total[k][:, rows * t : rows * (t + 1)]

        @pl.when(me == t)
        def _(t=t):
            for part in range(3):
                owner, slot = divmod(4 * part + t, 3)
                for h in range(n_h):
                    a = HEAD_DIM * (2 * h + part) if part < 2 else 2 * rows + HEAD_DIM * h
                    b = rows * slot + HEAD_DIM * h
                    vecs[owner, 1:2, b : b + HEAD_DIM] = bsum[:, a : a + HEAD_DIM]
            vecs[t, 1:2, 3 * rows : 4 * rows] = csum[:, rows * t : rows * (t + 1)]
            vecs[t, 2:3, :] = bup[...]

    for j in range(4):
        target = keep if j % 2 == 0 else send
        target[j // 2, 2 * count :, :] = vecs[me ^ j].astype(BF)


def add_kernel(kept, got, out):
    out[...] = (as_float(kept[...]) + as_float(got[...])).astype(out.dtype)


def add_one_kernel(kept, got, out):
    out[...] = (as_float(kept[1]) + as_float(got[1])).astype(BF)


def add_split_kernel(bit, kept, got, more, send, keep):
    mine = bit_of("rep", bit)
    for place, out in ((1 - mine, send), (mine, keep)):
        out[...] = (as_float(kept[place]) + as_float(got[place]) + as_float(more[place])).astype(BF)


def add_pieces_kernel(kept, got, more, p0, p1, p2, p3, *rest):
    me = lax.axis_index("shard")
    cols = p0.shape[1]
    for k, p in enumerate((p0, p1, p2, p3)):
        t = me ^ k
        total = (as_float(kept[t]) + as_float(got[t]) + as_float(more[t])).astype(BF)
        p[...] = total[:, :cols]
        if rest:
            rest[0][t] = total[:, cols:]


def pieces_split_kernel(bit, p0, p1, p2, p3, *rest):
    me = lax.axis_index("shard")
    mine = bit_of("rep", bit)
    send, keep = rest[-2:]
    cols = p0.shape[1]
    for k, p in enumerate((p0, p1, p2, p3)):
        s = me ^ k
        pair, slot = s >> 1, s & 1
        for target, wanted in ((keep, mine), (send, 1 - mine)):

            @pl.when(pair == wanted)
            def _(target=target):
                target[slot, :, :cols] = p[...]
                if len(rest) > 2:
                    target[slot, :, cols:] = rest[0][s]


def last_kernel(kept, got, vec, out):
    n, n_r, _ = kept.shape
    for k in range(n):
        out[n_r * k : n_r * (k + 1), :] = (as_float(kept[k]) + as_float(got[k])).astype(BF)
    out[n_r * n :, :] = vec[...]


def pair_vec_kernel(bit, own, got, out):
    mine = bit_of("rep", bit)
    n = (out.shape[0] - own.shape[0])
    out[pl.ds(pl.multiple_of(mine * n, 16), n), :] = own[:n, :]
    out[pl.ds(pl.multiple_of((1 - mine) * n, 16), n), :] = got[:n, :]
    out[2 * n :, :] = (as_float(own[n:, :]) + as_float(got[n:, :])).astype(BF)


def pair_kernel(bit, own, got, out):
    mine = bit_of("rep", bit)
    out[mine] = own[...]
    out[1 - mine] = got[...]


def quarters(order, refs):
    first, second = (bit_of("rep", bit) for bit in order)
    return zip(refs, (first, first, 1 - first, 1 - first), (second, 1 - second, second, 1 - second))


def final_down_kernel(order, p0, p1, p2, p3, out):
    for value, half, b in quarters(order, (p0, p1, p2, p3)):
        n_t, n_r, _ = value.shape
        for t in range(n_t):
            start = pl.multiple_of(((half * 2 + b) * n_t + t) * n_r, 8)
            out[pl.ds(start, n_r), :] = as_float(value[t])


def final_up_kernel(order, p0, p1, p2, p3, out, vec):
    n_r = out.shape[0] // 4
    wide = out.shape[1] // 4
    v0, v1, v2, v3 = (as_float(p[4 * n_r :, :]) for p in (p0, p1, p2, p3))
    vec[...] = (v0 + v1) + (v2 + v3)
    for value, half, b in quarters(order, (p0, p1, p2, p3)):
        start = pl.multiple_of((half * 2 + b) * n_r, 8)
        for s in range(4):
            out[pl.ds(start, n_r), wide * s : wide * (s + 1)] = as_float(value[n_r * s : n_r * (s + 1), :])


def final_qkv_kernel(order, p0, p1, p2, p3, out, out_w):
    rows = out_w.shape[0]
    n_h = rows // HEAD_DIM
    for value, half, b in quarters(order, (p0, p1, p2, p3)):
        n_s, n_r, width = value.shape
        place = pl.ds(pl.multiple_of((half * 2 + b) * n_r, 8), n_r)
        for s in range(n_s):
            block = as_float(value[s])
            for h in range(n_h):
                a = rows * s + HEAD_DIM * h
                two = 2 * HEAD_DIM * h
                out[place, a : a + HEAD_DIM] = block[:, two : two + HEAD_DIM]
                out[place, width + a : width + a + HEAD_DIM] = block[:, two + HEAD_DIM : two + 2 * HEAD_DIM]
            out[place, 2 * width + rows * s : 2 * width + rows * (s + 1)] = block[:, 2 * rows : 3 * rows]
            out_w[place, rows * s : rows * (s + 1)] = block[:, 3 * rows :]


def make_body(shards, reps):
    def body(
        block_input,
        positions,
        segments,
        w_qkv,
        b_qkv,
        w_out,
        b_out,
        w_up,
        b_up,
        w_down,
        b_down,
        ln1_gain,
        ln1_bias,
        ln2_gain,
        ln2_bias,
        cotangent,
    ):
        tokens_in = block_input[0]
        cotan_own = cotangent[0]
        count, width = tokens_in.shape
        length = segments.shape[1]
        rows = w_qkv.shape[0]
        wide = w_up.shape[1] // shards
        bits = powers(reps)

        def to(j, value):
            return swap(value, "shard", shards, j)

        def gather(value):
            two = to(2, value)
            one = to(1, value)
            return value, one, two, swap(two, "shard", shards, 1)

        x = gather(tokens_in)
        packed = call(
            pack_kernel,
            [((rows, 3 * rows), BF)] * 4 + [((rows, wide), BF)] * 4 + [((8, 3 * rows), F32)],
            (w_qkv, w_up, positions, ln1_gain, ln1_bias, ln2_gain, ln2_bias, b_out, b_down, b_qkv),
            scratch=[((4, rows, 3 * rows), BF)],
            limit=62,
        )
        q_w = (packed[0], *(to(j, packed[j]) for j in (1, 2, 3)))
        c = gather(cotan_own)
        u_w = (packed[4], *(to(j, packed[4 + j]) for j in (1, 2, 3)))

        small = gather(packed[8])
        first, second, third = bits[:3]
        order_att, order_down, order_up = (first, second), (first, second), (second, first)
        sub = rows // 4
        n_c = width // rows

        hid1, hid1_t, hid2, hid2_t, cot, dact, datt, csum, vec_in, bias_qkv, position_all = call(
            prep_kernel,
            [((length, width), BF), ((width, length), BF)] * 2
            + [((length, width), BF), ((length, wide), F32), ((length, rows), BF), ((1, width), F32)]
            + [((8, width), F32), ((1, 3 * rows), F32), ((1, length), F32)],
            (*x, *c, *small, w_down, w_out),
            scratch=[((4, 8, 3 * rows), F32), ((1, 3 * width), F32)],
            flops=1_000_000_000,
            limit=24,
        )
        half = ROT // 2
        lane = jnp.arange(2 * HEAD_DIM) % HEAD_DIM
        freqs = jnp.exp((lane % half).astype(F32) * (-math.log(10000.0) / half))
        angles = position_all.reshape(-1, 1) * freqs[None, :]
        cosine, sine = jnp.cos(angles), jnp.sin(angles)
        ca = jnp.where(lane < ROT, cosine, 1.0)
        sa = jnp.where(lane < half, -sine, 0.0)
        sb = jnp.where((lane >= half) & (lane < ROT), sine, 0.0)

        *grad_a, activ, slope, wu_full = call(
            lambda *refs: mlp1_kernel(order_down, *refs),
            [((2, wide // 8, width), BF)] * 4
            + [((length, wide), BF), ((length, wide), F32), ((width, wide), BF)],
            (hid2, cot, *u_w, as_float(b_up).reshape(1, -1)),
            scratch=[((wide, width), BF)],
            flops=2_000_000_000,
            limit=24,
        )
        *grad_b, dpre, bup_sum = call(
            lambda *refs: mlp2_kernel(order_up, *refs),
            [((shards, sub, wide), BF)] * 4 + [((length, wide), BF), ((1, wide), F32)],
            (dact, hid2_t, slope),
            scratch=[((width, wide), BF)],
            flops=2_000_000_000,
            limit=24,
        )
        *grad_c, att, dproj, wq_full, bsum = call(
            lambda *refs: att_kernel(order_att, *refs),
            [((n_c, sub, width), BF)] * 4
            + [
                ((length, rows), BF),
                ((length, 3 * rows), BF),
                ((width, 3 * rows), BF),
                ((1, 3 * rows), F32),
            ],
            (hid1, hid1_t, cot, datt, *q_w, bias_qkv, ca, sa, sb, segments.reshape(-1, 1), segments),
            scratch=[((length, length), F32), ((width, width), BF)],
            flops=4_000_000_000,
            limit=24,
        )
        rs_send, rs_keep = call(
            mlp3_kernel,
            [((2, 2 * count + 16, width), BF)] * 2,
            (*x, att, activ, dproj, dpre, w_out, w_down, wq_full, wu_full, vec_in,
             bsum, csum, bup_sum),
            scratch=[((4, 16, width), F32)],
            flops=3_000_000_000,
            limit=24,
        )

        def over(bit, value):
            return swap(value, "rep", reps, bit)

        got = to(1, rs_send)
        (onward,) = call(add_one_kernel, [(got.shape[1:], BF)], (rs_keep, got))
        total = as_float(rs_keep[0]) + as_float(got[0]) + as_float(to(2, onward))
        output = as_float(tokens_in) + total[:count] + vec_in[4:5] + vec_in[5:6]
        d_norm = total[count : 2 * count]
        vec_own = total[2 * count :].astype(BF)
        own_normed, inv_std = normalize(as_float(tokens_in))
        d_input = as_float(cotan_own) + inv_std * (
            d_norm
            - jnp.mean(d_norm, axis=-1, keepdims=True)
            - own_normed * jnp.mean(d_norm * own_normed, axis=-1, keepdims=True)
        )

        def start_sum(bit_order, grad):
            sent_a, sent_b, kept_a, kept_b = grad
            one, two = bit_order
            got_a = over(one, sent_a)
            got_b = over(one, sent_b)
            (sent,) = call(add_kernel, [(kept_a.shape, BF)], (kept_a, got_a))
            return kept_b, got_b, over(two, sent)

        def finish_sum(bit_order, sent, kept, shape, vec=None):
            one, two = bit_order
            got = over(third, sent)
            if vec is None:
                (own,) = call(add_kernel, [(kept.shape, BF)], (kept, got))
            else:
                n_rows = kept.shape[0] * kept.shape[1]
                shape = (2 * n_rows + vec.shape[0], shape[2])
                (own,) = call(last_kernel, [((n_rows + vec.shape[0], shape[1]), BF)], (kept, got, vec))
            for bit in bits[3:]:
                more = over(bit, own)
                (own,) = call(add_kernel, [(own.shape, BF)], (own, more))
            (both,) = call(
                lambda *refs: (pair_kernel if vec is None else pair_vec_kernel)(third, *refs),
                [((2, *own.shape) if vec is None else shape, BF)],
                (own, over(third, own)),
            )
            both = both.reshape(shape)
            other = over(two, both)
            return both, other, over(one, both), over(one, other)

        def shard_stream(bit_order, grad, cols, vec=None):
            held = start_sum(bit_order, grad)
            shape = held[0].shape
            extra = [] if cols == shape[2] else [((n_c, sub, shape[2] - cols), BF)]
            parts = call(add_pieces_kernel, [((sub, cols), BF)] * 4 + extra, held)
            mixed = (parts[0], *(to(j, parts[j]) for j in range(1, 4)), *parts[4:])
            sent, kept = call(lambda *refs: pieces_split_kernel(third, *refs), [((2, sub, shape[2]), BF)] * 2, mixed)
            return finish_sum(bit_order, sent, kept, shape, vec)

        def plain_stream(bit_order, grad):
            held = start_sum(bit_order, grad)
            shape = held[0].shape
            sent, kept = call(lambda *refs: add_split_kernel(third, *refs), [(shape[1:], BF)] * 2, held)
            return finish_sum(bit_order, sent, kept, shape)

        own_c = shard_stream(order_att, grad_c, 3 * rows)
        own_a = plain_stream(order_down, grad_a)
        own_b = shard_stream(order_up, grad_b, wide, vec_own)
        tot_qkv, tot_out = call(
            lambda *refs: final_qkv_kernel(order_att, *refs), [((rows, 3 * width), F32), ((rows, width), F32)], own_c
        )
        (tot_down,) = call(lambda *refs: final_down_kernel(order_down, *refs), [((wide, width), F32)], own_a)
        tot_up, vec = call(
            lambda *refs: final_up_kernel(order_up, *refs), [((rows, shards * wide), F32), (vec_own.shape, F32)], own_b
        )

        g1, bb1, g2, bb2 = [vec[0, k * rows : (k + 1) * rows] for k in range(4)]
        tot_bqkv = vec[1, : 3 * rows]
        tot_cot = vec[1, 3 * rows :]
        tot_bup = vec[2]
        return (
            output[None],
            d_input[None],
            tot_qkv,
            tot_bqkv,
            tot_out,
            tot_cot,
            tot_up,
            tot_bup,
            tot_down,
            tot_cot,
            g1,
            bb1,
            g2,
            bb2,
        )

    return body


def solution(mesh):
    body = make_body(mesh.shape["shard"], mesh.shape["rep"])
    return jax.shard_map(
        body,
        mesh=mesh,
        in_specs=(
            P("rep", "shard", None),
            P("rep", "shard"),
            P("rep", None),
            P("shard", None),
            P("shard"),
            P("shard", None),
            P("shard"),
            P("shard", None),
            P("shard"),
            P("shard", None),
            P("shard"),
            P("shard"),
            P("shard"),
            P("shard"),
            P("shard"),
            P("rep", "shard", None),
        ),
        out_specs=(
            P("rep", "shard", None),
            P("rep", "shard", None),
            P("shard", None),
            P("shard"),
            P("shard", None),
            P("shard"),
            P("shard", None),
            P("shard"),
            P("shard", None),
            P("shard"),
            P("shard"),
            P("shard"),
            P("shard"),
            P("shard"),
        ),
        check_vma=False,
    )
```

```python
import math

import jax
import jax.numpy as jnp
from jax import lax
from jax.experimental import pallas as pl
from jax.experimental.pallas import tpu as pltpu
from jax.sharding import PartitionSpec as P


HEAD_DIM = 64
ROT = 16

EPSILON = 1e-05
INV_ROOT_TWO = 0.7071067811865476
INV_ROOT_TWO_PI = 0.3989422804014327


BF = jnp.bfloat16
F32 = jnp.float32


def as_float(array_in):
    return array_in.astype(F32)


def dot(left, right, dims):
    return lax.dot_general(left, right, (dims, ((), ())), preferred_element_type=F32)


def normalize(values):
    centre = values - jnp.mean(values, axis=-1, keepdims=True)
    inv_std = lax.rsqrt(jnp.mean(centre * centre, axis=-1, keepdims=True) + EPSILON)
    return (centre * inv_std, inv_std)


def gelu_parts(pre_act):
    cdf = 0.5 * (1.0 + lax.erf(pre_act * INV_ROOT_TWO))
    return pre_act * cdf, cdf + pre_act * jnp.exp(-0.5 * pre_act * pre_act) * INV_ROOT_TWO_PI


def swap(value, axis, size, bit):
    return lax.ppermute(value, axis, [(i, i ^ bit) for i in range(size)])


def powers(size):
    return [1 << k for k in range(size.bit_length() - 1)]


def call(kernel, outs, ins, scratch=(), flops=0, limit=8):
    shapes = [jax.ShapeDtypeStruct(s, d) for s, d in outs]
    moved = sum(math.prod(v.shape) * v.dtype.itemsize for v in [*ins, *shapes])
    return pl.pallas_call(
        kernel,
        out_shape=shapes,
        scratch_shapes=[pltpu.VMEM(s, d) for s, d in scratch],
        compiler_params=pltpu.CompilerParams(vmem_limit_bytes=limit * 1024 * 1024),
        cost_estimate=pl.CostEstimate(flops=flops, bytes_accessed=moved, transcendentals=0),
    )(*ins)


def bit_of(axis, bit):
    return jnp.where((lax.axis_index(axis) & bit) != 0, 1, 0).astype(jnp.int32)


def pack_kernel(wq, wu, pos, g1, b1, g2, b2, bo, bd, bq, q0, q1, q2, q3, u0, u1, u2, u3, small, scr):
    me = lax.axis_index("shard")
    rows = wq.shape[0]
    count = pos.shape[1]
    for k, ref in enumerate((g1, b1, g2, b2, bo, bd)):
        small[k : k + 1, :rows] = as_float(ref[...]).reshape(1, rows)
    small[6:7, : 3 * rows] = as_float(bq[...]).reshape(1, 3 * rows)
    small[7:8, :count] = as_float(pos[...])
    width = wq.shape[1] // 3
    wide = u0.shape[1]
    n_h = rows // HEAD_DIM
    for t in range(4):
        base = rows * t
        for h in range(n_h):
            a = base + HEAD_DIM * h
            scr[t, :, 2 * HEAD_DIM * h : 2 * HEAD_DIM * h + HEAD_DIM] = wq[:, a : a + HEAD_DIM]
            scr[t, :, 2 * HEAD_DIM * h + HEAD_DIM : 2 * HEAD_DIM * (h + 1)] = wq[
                :, width + a : width + a + HEAD_DIM
            ]
        scr[t, :, 2 * rows : 3 * rows] = wq[:, 2 * width + base : 2 * width + base + rows]
    half = q2.shape[0]
    mine = pl.ds(pl.multiple_of(bit_of("rep", 1) * half, 16), half)
    for k, (q, u) in enumerate(((q0, u0), (q1, u1), (q2, u2), (q3, u3))):
        t = me ^ k
        q[...] = scr[t] if k < 2 else scr[t, mine, :]
        u[...] = wu[:, pl.ds(pl.multiple_of(t * wide, 128), wide)]


def normed_of(ref):
    return normalize(ref[...].astype(F32))[0]


def write_rows(targets, grid, first, second, place):
    for target, half, b in zip(
        targets, (1 - first, 1 - first, first, first), (1 - second, second, 1 - second, second)
    ):
        n_t, n_r, _ = target.shape
        for t in range(n_t):
            start = pl.multiple_of(place(half, b, t), 16)
            target[t] = grid[pl.ds(start, n_r), :]


def prep_kernel(x0, x1, x2, x3, c0, c1, c2, c3, s0, s1, s2, s3, wd, wo,
                hid1, hid1_t, hid2, hid2_t, cot, dact, datt, csum, vec, bq_own, pos, sm, bq):
    me = lax.axis_index("shard")
    count = x0.shape[0]
    rows = wo.shape[0]
    width = wo.shape[1]
    for j, ref in enumerate((s0, s1, s2, s3)):
        sm[me ^ j] = ref[...]
    vec[...] = jnp.zeros_like(vec)
    for s in range(4):
        for k in range(6):
            vec[k : k + 1, rows * s : rows * (s + 1)] = sm[s, k : k + 1, :rows]
        bq[:, 3 * rows * s : 3 * rows * (s + 1)] = sm[s, 6:7, :]
        pos[:, count * s : count * (s + 1)] = sm[s, 7:8, :count]
    for t in range(4):

        @pl.when(me == t)
        def _(t=t):
            for part in range(3):
                for h in range(rows // HEAD_DIM):
                    a = part * width + rows * t + HEAD_DIM * h
                    b = HEAD_DIM * (2 * h + part) if part < 2 else 2 * rows + HEAD_DIM * h
                    bq_own[:, b : b + HEAD_DIM] = bq[:, a : a + HEAD_DIM]

    gain1, bias1, gain2, bias2 = (vec[k : k + 1, :] for k in range(4))
    for j, (x, c) in enumerate(((x0, c0), (x1, c1), (x2, c2), (x3, c3))):
        place = pl.ds(pl.multiple_of((me ^ j) * count, count), count)
        normed = normed_of(x)
        hid1[place, :] = (normed * gain1 + bias1).astype(BF)
        hid2[place, :] = (normed * gain2 + bias2).astype(BF)
        cot[place, :] = c[...]
    hid1_t[...] = hid1[...].T
    hid2_t[...] = hid2[...].T
    dact[...] = dot(cot[...], wd[...], ((1,), (1,)))
    datt[...] = dot(cot[...], wo[...], ((1,), (1,))).astype(BF)
    csum[...] = jnp.sum(as_float(cot[...]), axis=0, keepdims=True)


def att_kernel(order, hid, hid_t, cot, datt, q0, q1, q2, q2r, q3, q3r, bq, ca, sa, sb, segc, segr,
               sa_o, sb_o, ka_o, kb_o, att_o, dproj_o, wfull, bsum, neg, grid):
    me = lax.axis_index("shard")
    first, second = (bit_of("rep", bit) for bit in order)
    rows = q0.shape[0]
    length, width = cot.shape
    two = 2 * HEAD_DIM
    n_h = rows // HEAD_DIM
    side = bit_of("rep", 1)
    for j, part, q in ((0, 0, q0), (1, 0, q1), (2, side, q2), (2, 1 - side, q2r), (3, side, q3), (3, 1 - side, q3r)):
        n = q.shape[0]
        wfull[pl.ds(pl.multiple_of((me ^ j) * rows + part * n, 16), n), :] = q[...]
    col = lax.broadcasted_iota(jnp.int32, (length, length), 1)
    row = lax.broadcasted_iota(jnp.int32, (length, length), 0)
    neg[...] = jnp.where((col <= row) & (segc[...] == segr[...]), 0.0, -jnp.inf)
    proj = dot(hid[...], wfull[...], ((1,), (0,))) + bq[...]
    for h in range(n_h):
        qk = proj[:, two * h : two * (h + 1)]
        qk = qk * ca[...] + pltpu.roll(qk, two - ROT // 2, 1) * sa[...] + pltpu.roll(qk, ROT // 2, 1) * sb[...]
        qk = qk.astype(BF)
        query, key = qk[:, :HEAD_DIM], qk[:, HEAD_DIM:]
        vals = slice(2 * rows + HEAD_DIM * h, 2 * rows + HEAD_DIM * (h + 1))
        val = proj[:, vals].astype(BF)
        da = datt[:, HEAD_DIM * h : HEAD_DIM * (h + 1)]
        scores = dot(query * jnp.asarray(0.125, BF), key, ((1,), (1,))) + neg[...]
        top = jnp.max(scores, axis=-1, keepdims=True)
        expo = jnp.exp(scores - top)
        prob = expo * (1.0 / jnp.sum(expo, axis=-1, keepdims=True))
        prob_b = prob.astype(BF)
        att = dot(prob_b, val, ((1,), (0,))).astype(BF)
        att_o[:, HEAD_DIM * h : HEAD_DIM * (h + 1)] = att
        d_val = dot(prob_b, da, ((0,), (0,)))
        d_prob = dot(da, val, ((1,), (1,)))
        row_dot = jnp.sum(as_float(da) * as_float(att), axis=-1, keepdims=True)
        d_score = (prob * (d_prob - row_dot)).astype(BF)
        dqk = 0.125 * jnp.concatenate(
            [dot(d_score, key, ((1,), (0,))), dot(d_score, query, ((0,), (0,)))], axis=1
        )
        dqk = dqk * ca[...] - pltpu.roll(dqk, two - ROT // 2, 1) * sa[...] - pltpu.roll(dqk, ROT // 2, 1) * sb[...]
        dproj_o[:, two * h : two * (h + 1)] = dqk.astype(BF)
        dproj_o[:, vals] = d_val.astype(BF)
        bsum[:, two * h : two * (h + 1)] = jnp.sum(dqk, axis=0, keepdims=True)
        bsum[:, vals] = jnp.sum(d_val, axis=0, keepdims=True)
    grid[:, : 3 * rows] = dot(hid_t[...], dproj_o[...], ((1,), (0,))).astype(BF)
    g_out = dot(att_o[...], cot[...], ((0,), (0,))).astype(BF)
    for t in range(width // rows):
        grid[rows * t : rows * (t + 1), 3 * rows :] = g_out[:, rows * t : rows * (t + 1)]
    n_r = sa_o.shape[1]
    write_rows(
        (sa_o, sb_o, ka_o, kb_o), grid, first, second, lambda half, b, t: t * rows + (2 * half + b) * n_r
    )


def mlp1_kernel(order, hid, cot, u0, u1, u2, u3, bup, sa_o, sb_o, ka_o, kb_o, activ, slope, wfull, grid):
    me = lax.axis_index("shard")
    first, second = (bit_of("rep", bit) for bit in order)
    rows = u0.shape[0]
    for j, u in enumerate((u0, u1, u2, u3)):
        wfull[pl.ds(pl.multiple_of((me ^ j) * rows, 16), rows), :] = u[...]
    block = hid.shape[0] // 4
    for j in range(4):
        part = slice(block * j, block * (j + 1))
        pre_act = dot(hid[part, :], wfull[...], ((1,), (0,))) + bup[...]
        act, slp = gelu_parts(pre_act)
        activ[part, :] = act.astype(BF)
        slope[part, :] = slp
    grid[...] = dot(activ[...], cot[...], ((0,), (0,))).astype(BF)
    n_t, n_r, _ = sa_o.shape
    write_rows(
        (sa_o, sb_o, ka_o, kb_o), grid, first, second, lambda half, b, t: ((half * 2 + b) * n_t + t) * n_r
    )


def mlp2_kernel(order, dact, hid_t, slope, sa_o, sb_o, ka_o, kb_o, dpre, bsum, grid):
    first, second = (bit_of("rep", bit) for bit in order)
    d_pre = dact[...] * slope[...]
    dpre[...] = d_pre.astype(BF)
    bsum[...] = jnp.sum(d_pre, axis=0, keepdims=True)
    grid[...] = dot(hid_t[...], dpre[...], ((1,), (0,))).astype(BF)
    n_r = sa_o.shape[1]
    rows = n_r * 4
    write_rows(
        (sa_o, sb_o, ka_o, kb_o), grid, first, second, lambda half, b, t: t * rows + (2 * half + b) * n_r
    )


def mlp3_kernel(x0, x1, x2, x3, att, activ, dproj, dpre, wo, wd, wq, wu, vec,
                bsum, csum, bup, send, keep, vecs, out_s, one_s, two_s):
    me = lax.axis_index("shard")
    count = x0.shape[0]
    total = [None] * 4
    out_s[...] = dot(att[...], wo[...], ((1,), (0,))) + dot(activ[...], wd[...], ((1,), (0,)))
    one_s[...] = dot(dproj[...], wq[...], ((1,), (1,)))
    two_s[...] = dot(dpre[...], wu[...], ((1,), (1,)))
    for j, x in enumerate((x0, x1, x2, x3)):
        part = pl.ds(pl.multiple_of((me ^ j) * count, count), count)
        out, one, two = out_s[part, :], one_s[part, :], two_s[part, :]
        normed = normed_of(x)
        target = keep if j % 2 == 0 else send
        target[j // 2, :count, :] = out.astype(BF)
        target[j // 2, count : 2 * count, :] = (one * vec[0:1, :] + two * vec[2:3, :]).astype(BF)
        for k, value in enumerate((one * normed, one, two * normed, two)):
            piece = jnp.sum(value, axis=0, keepdims=True)
            total[k] = piece if total[k] is None else total[k] + piece
    rows, _ = wo.shape
    n_h = rows // HEAD_DIM
    vecs[...] = jnp.zeros_like(vecs)
    for t in range(4):
        for k in range(4):
            vecs[t, 0:1, rows * k : rows * (k + 1)] = total[k][:, rows * t : rows * (t + 1)]

        @pl.when(me == t)
        def _(t=t):
            for part in range(3):
                owner, slot = divmod(4 * part + t, 3)
                for h in range(n_h):
                    a = HEAD_DIM * (2 * h + part) if part < 2 else 2 * rows + HEAD_DIM * h
                    b = rows * slot + HEAD_DIM * h
                    vecs[owner, 1:2, b : b + HEAD_DIM] = bsum[:, a : a + HEAD_DIM]
            vecs[t, 1:2, 3 * rows : 4 * rows] = csum[:, rows * t : rows * (t + 1)]
            vecs[t, 2:3, :] = bup[...]

    for j in range(4):
        target = keep if j % 2 == 0 else send
        target[j // 2, 2 * count :, :] = vecs[me ^ j].astype(BF)


def add_kernel(kept, got, out):
    out[...] = (as_float(kept[...]) + as_float(got[...])).astype(out.dtype)


def add_one_kernel(kept, got, out):
    out[...] = (as_float(kept[1]) + as_float(got[1])).astype(BF)


def add_split_kernel(bit, kept, got, more, send, keep):
    mine = bit_of("rep", bit)
    for place, out in ((1 - mine, send), (mine, keep)):
        out[...] = (as_float(kept[place]) + as_float(got[place]) + as_float(more[place])).astype(BF)


def add_pieces_kernel(kept, got, more, p0, p1, p2, p3, *rest):
    me = lax.axis_index("shard")
    cols = p0.shape[1]
    for k, p in enumerate((p0, p1, p2, p3)):
        t = me ^ k
        total = (as_float(kept[t]) + as_float(got[t]) + as_float(more[t])).astype(BF)
        p[...] = total[:, :cols]
        if rest:
            rest[0][t] = total[:, cols:]


def pieces_split_kernel(bit, p0, p1, p2, p3, *rest):
    me = lax.axis_index("shard")
    mine = bit_of("rep", bit)
    send, keep = rest[-2:]
    cols = p0.shape[1]
    for k, p in enumerate((p0, p1, p2, p3)):
        s = me ^ k
        pair, slot = s >> 1, s & 1
        for target, wanted in ((keep, mine), (send, 1 - mine)):

            @pl.when(pair == wanted)
            def _(target=target):
                target[slot, :, :cols] = p[...]
                if len(rest) > 2:
                    target[slot, :, cols:] = rest[0][s]


def last_kernel(kept, got, vec, out):
    n, n_r, _ = kept.shape
    for k in range(n):
        out[n_r * k : n_r * (k + 1), :] = (as_float(kept[k]) + as_float(got[k])).astype(BF)
    out[n_r * n :, :] = vec[...]


def pair_vec_kernel(bit, own, got, out):
    mine = bit_of("rep", bit)
    n = (out.shape[0] - own.shape[0])
    out[pl.ds(pl.multiple_of(mine * n, 16), n), :] = own[:n, :]
    out[pl.ds(pl.multiple_of((1 - mine) * n, 16), n), :] = got[:n, :]
    out[2 * n :, :] = (as_float(own[n:, :]) + as_float(got[n:, :])).astype(BF)


def pair_kernel(bit, own, got, out):
    mine = bit_of("rep", bit)
    out[mine] = own[...]
    out[1 - mine] = got[...]


def quarters(order, refs):
    first, second = (bit_of("rep", bit) for bit in order)
    return zip(refs, (first, first, 1 - first, 1 - first), (second, 1 - second, second, 1 - second))


def final_down_kernel(order, p0, p1, p2, p3, out):
    for value, half, b in quarters(order, (p0, p1, p2, p3)):
        n_t, n_r, _ = value.shape
        for t in range(n_t):
            start = pl.multiple_of(((half * 2 + b) * n_t + t) * n_r, 8)
            out[pl.ds(start, n_r), :] = as_float(value[t])


def final_up_kernel(order, p0, p1, p2, p3, out, g1, b1, g2, b2, tot_q, cot_a, cot_b, tot_u, vec):
    n_r = out.shape[0] // 4
    wide = out.shape[1] // 4
    v0, v1, v2, v3 = (as_float(p[4 * n_r :, :]) for p in (p0, p1, p2, p3))
    vec[...] = (v0 + v1) + (v2 + v3)
    rows = g1.shape[0]
    for k, ref in enumerate((g1, b1, g2, b2)):
        ref[...] = vec[0, rows * k : rows * (k + 1)]
    tot_q[...] = vec[1, : 3 * rows]
    cot_a[...] = vec[1, 3 * rows :]
    cot_b[...] = vec[1, 3 * rows :]
    tot_u[...] = vec[2, :]
    for value, half, b in quarters(order, (p0, p1, p2, p3)):
        start = pl.multiple_of((half * 2 + b) * n_r, 8)
        for s in range(4):
            out[pl.ds(start, n_r), wide * s : wide * (s + 1)] = as_float(value[n_r * s : n_r * (s + 1), :])


def final_qkv_kernel(order, p0, p1, p2, p3, out, out_w):
    rows = out_w.shape[0]
    n_h = rows // HEAD_DIM
    for value, half, b in quarters(order, (p0, p1, p2, p3)):
        n_s, n_r, width = value.shape
        place = pl.ds(pl.multiple_of((half * 2 + b) * n_r, 8), n_r)
        for s in range(n_s):
            block = as_float(value[s])
            for h in range(n_h):
                a = rows * s + HEAD_DIM * h
                two = 2 * HEAD_DIM * h
                out[place, a : a + HEAD_DIM] = block[:, two : two + HEAD_DIM]
                out[place, width + a : width + a + HEAD_DIM] = block[:, two + HEAD_DIM : two + 2 * HEAD_DIM]
            out[place, 2 * width + rows * s : 2 * width + rows * (s + 1)] = block[:, 2 * rows : 3 * rows]
            out_w[place, rows * s : rows * (s + 1)] = block[:, 3 * rows :]


def make_body(shards, reps):
    def body(
        block_input,
        positions,
        segments,
        w_qkv,
        b_qkv,
        w_out,
        b_out,
        w_up,
        b_up,
        w_down,
        b_down,
        ln1_gain,
        ln1_bias,
        ln2_gain,
        ln2_bias,
        cotangent,
    ):
        tokens_in = block_input[0]
        cotan_own = cotangent[0]
        count, width = tokens_in.shape
        length = segments.shape[1]
        rows = w_qkv.shape[0]
        wide = w_up.shape[1] // shards
        bits = powers(reps)

        def to(j, value):
            return swap(value, "shard", shards, j)

        def gather(value):
            two = to(2, value)
            one = to(1, value)
            return value, one, two, swap(two, "shard", shards, 1)

        x = gather(tokens_in)
        packed = call(
            pack_kernel,
            [((rows, 3 * rows), BF)] * 2
            + [((rows // 2, 3 * rows), BF)] * 2
            + [((rows, wide), BF)] * 4
            + [((8, 3 * rows), F32)],
            (w_qkv, w_up, positions, ln1_gain, ln1_bias, ln2_gain, ln2_bias, b_out, b_down, b_qkv),
            scratch=[((4, rows, 3 * rows), BF)],
            limit=62,
        )
        q_two, q_three = to(2, packed[2]), to(3, packed[3])
        q_w = (packed[0], to(1, packed[1]), q_two, swap(q_two, "rep", reps, 1), q_three, swap(q_three, "rep", reps, 1))
        c = gather(cotan_own)
        u_w = (packed[4], *(to(j, packed[4 + j]) for j in (1, 2, 3)))

        small = gather(packed[8])
        first, second, third = bits[:3]
        order_att, order_down, order_up = (first, second), (second, first), (first, second)
        sub = rows // 4
        n_c = width // rows

        hid1, hid1_t, hid2, hid2_t, cot, dact, datt, csum, vec_in, bias_qkv, position_all = call(
            prep_kernel,
            [((length, width), BF), ((width, length), BF)] * 2
            + [((length, width), BF), ((length, wide), F32), ((length, rows), BF), ((1, width), F32)]
            + [((8, width), F32), ((1, 3 * rows), F32), ((1, length), F32)],
            (*x, *c, *small, w_down, w_out),
            scratch=[((4, 8, 3 * rows), F32), ((1, 3 * width), F32)],
            flops=1_000_000_000,
            limit=24,
        )
        half = ROT // 2
        lane = jnp.arange(2 * HEAD_DIM) % HEAD_DIM
        freqs = jnp.exp((lane % half).astype(F32) * (-math.log(10000.0) / half))
        angles = position_all.reshape(-1, 1) * freqs[None, :]
        cosine, sine = jnp.cos(angles), jnp.sin(angles)
        ca = jnp.where(lane < ROT, cosine, 1.0)
        sa = jnp.where(lane < half, -sine, 0.0)
        sb = jnp.where((lane >= half) & (lane < ROT), sine, 0.0)

        *grad_a, activ, slope, wu_full = call(
            lambda *refs: mlp1_kernel(order_down, *refs),
            [((2, wide // 8, width), BF)] * 4
            + [((length, wide), BF), ((length, wide), F32), ((width, wide), BF)],
            (hid2, cot, *u_w, as_float(b_up).reshape(1, -1)),
            scratch=[((wide, width), BF)],
            flops=2_000_000_000,
            limit=24,
        )
        *grad_b, dpre, bup_sum = call(
            lambda *refs: mlp2_kernel(order_up, *refs),
            [((shards, sub, wide), BF)] * 4 + [((length, wide), BF), ((1, wide), F32)],
            (dact, hid2_t, slope),
            scratch=[((width, wide), BF)],
            flops=2_000_000_000,
            limit=24,
        )
        *grad_c, att, dproj, wq_full, bsum = call(
            lambda *refs: att_kernel(order_att, *refs),
            [((n_c, sub, width), BF)] * 4
            + [
                ((length, rows), BF),
                ((length, 3 * rows), BF),
                ((width, 3 * rows), BF),
                ((1, 3 * rows), F32),
            ],
            (hid1, hid1_t, cot, datt, *q_w, bias_qkv, ca, sa, sb, segments.reshape(-1, 1), segments),
            scratch=[((length, length), F32), ((width, width), BF)],
            flops=4_000_000_000,
            limit=24,
        )
        rs_send, rs_keep = call(
            mlp3_kernel,
            [((2, 2 * count + 16, width), BF)] * 2,
            (*x, att, activ, dproj, dpre, w_out, w_down, wq_full, wu_full, vec_in,
             bsum, csum, bup_sum),
            scratch=[((4, 16, width), F32)] + [((length, width), F32)] * 3,
            flops=3_000_000_000,
            limit=24,
        )

        def over(bit, value):
            return swap(value, "rep", reps, bit)

        got = to(1, rs_send)
        (onward,) = call(add_one_kernel, [(got.shape[1:], BF)], (rs_keep, got))
        total = as_float(rs_keep[0]) + as_float(got[0]) + as_float(to(2, onward))
        output = as_float(tokens_in) + total[:count] + vec_in[4:5] + vec_in[5:6]
        d_norm = total[count : 2 * count]
        vec_own = total[2 * count :].astype(BF)
        own_normed, inv_std = normalize(as_float(tokens_in))
        d_input = as_float(cotan_own) + inv_std * (
            d_norm
            - jnp.mean(d_norm, axis=-1, keepdims=True)
            - own_normed * jnp.mean(d_norm * own_normed, axis=-1, keepdims=True)
        )

        def start_sum(bit_order, grad):
            sent_a, sent_b, kept_a, kept_b = grad
            one, two = bit_order
            got_a = over(one, sent_a)
            got_b = over(one, sent_b)
            (sent,) = call(add_kernel, [(kept_a.shape, BF)], (kept_a, got_a))
            return kept_b, got_b, over(two, sent)

        def finish_sum(bit_order, sent, kept, shape, vec=None):
            one, two = bit_order
            got = over(third, sent)
            if vec is None:
                (own,) = call(add_kernel, [(kept.shape, BF)], (kept, got))
            else:
                n_rows = kept.shape[0] * kept.shape[1]
                shape = (2 * n_rows + vec.shape[0], shape[2])
                (own,) = call(last_kernel, [((n_rows + vec.shape[0], shape[1]), BF)], (kept, got, vec))
            for bit in bits[3:]:
                more = over(bit, own)
                (own,) = call(add_kernel, [(own.shape, BF)], (own, more))
            (both,) = call(
                lambda *refs: (pair_kernel if vec is None else pair_vec_kernel)(third, *refs),
                [((2, *own.shape) if vec is None else shape, BF)],
                (own, over(third, own)),
            )
            both = both.reshape(shape)
            other = over(two, both)
            return both, other, over(one, both), over(one, other)

        def shard_stream(bit_order, grad, cols, vec=None):
            held = start_sum(bit_order, grad)
            shape = held[0].shape
            extra = [] if cols == shape[2] else [((n_c, sub, shape[2] - cols), BF)]
            parts = call(add_pieces_kernel, [((sub, cols), BF)] * 4 + extra, held)
            mixed = (parts[0], *(to(j, parts[j]) for j in range(1, 4)), *parts[4:])
            sent, kept = call(lambda *refs: pieces_split_kernel(third, *refs), [((2, sub, shape[2]), BF)] * 2, mixed)
            return finish_sum(bit_order, sent, kept, shape, vec)

        def plain_stream(bit_order, grad):
            held = start_sum(bit_order, grad)
            shape = held[0].shape
            sent, kept = call(lambda *refs: add_split_kernel(third, *refs), [(shape[1:], BF)] * 2, held)
            return finish_sum(bit_order, sent, kept, shape)

        own_c = shard_stream(order_att, grad_c, 3 * rows)
        own_a = plain_stream(order_down, grad_a)
        own_b = shard_stream(order_up, grad_b, wide, vec_own)
        tot_qkv, tot_out = call(
            lambda *refs: final_qkv_kernel(order_att, *refs), [((rows, 3 * width), F32), ((rows, width), F32)], own_c
        )
        (tot_down,) = call(lambda *refs: final_down_kernel(order_down, *refs), [((wide, width), F32)], own_a)
        tot_up, g1, bb1, g2, bb2, tot_bqkv, tot_cot, tot_cot_two, tot_bup = call(
            lambda *refs: final_up_kernel(order_up, *refs),
            [((rows, shards * wide), F32)]
            + [((n,), F32) for n in (rows, rows, rows, rows, 3 * rows, rows, rows, wide)],
            own_b,
            scratch=[(vec_own.shape, F32)],
        )

        return (
            output[None],
            d_input[None],
            tot_qkv,
            tot_bqkv,
            tot_out,
            tot_cot,
            tot_up,
            tot_bup,
            tot_down,
            tot_cot_two,
            g1,
            bb1,
            g2,
            bb2,
        )

    return body


def solution(mesh):
    body = make_body(mesh.shape["shard"], mesh.shape["rep"])
    return jax.shard_map(
        body,
        mesh=mesh,
        in_specs=(
            P("rep", "shard", None),
            P("rep", "shard"),
            P("rep", None),
            P("shard", None),
            P("shard"),
            P("shard", None),
            P("shard"),
            P("shard", None),
            P("shard"),
            P("shard", None),
            P("shard"),
            P("shard"),
            P("shard"),
            P("shard"),
            P("shard"),
            P("rep", "shard", None),
        ),
        out_specs=(
            P("rep", "shard", None),
            P("rep", "shard", None),
            P("shard", None),
            P("shard"),
            P("shard", None),
            P("shard"),
            P("shard", None),
            P("shard"),
            P("shard", None),
            P("shard"),
            P("shard"),
            P("shard"),
            P("shard"),
            P("shard"),
        ),
        check_vma=False,
    )
```

```python
import math

import jax
import jax.numpy as jnp
from jax import lax
from jax.experimental import pallas as pl
from jax.experimental.pallas import tpu as pltpu
from jax.sharding import PartitionSpec as P


HEAD_DIM = 64
ROT = 16

EPSILON = 1e-05
INV_ROOT_TWO = 0.7071067811865476
INV_ROOT_TWO_PI = 0.3989422804014327


BF = jnp.bfloat16
F32 = jnp.float32


def as_float(array_in):
    return array_in.astype(F32)


def dot(left, right, dims):
    return lax.dot_general(left, right, (dims, ((), ())), preferred_element_type=F32)


def normalize(values):
    centre = values - jnp.mean(values, axis=-1, keepdims=True)
    inv_std = lax.rsqrt(jnp.mean(centre * centre, axis=-1, keepdims=True) + EPSILON)
    return (centre * inv_std, inv_std)


def gelu_parts(pre_act):
    cdf = 0.5 * (1.0 + lax.erf(pre_act * INV_ROOT_TWO))
    return pre_act * cdf, cdf + pre_act * jnp.exp(-0.5 * pre_act * pre_act) * INV_ROOT_TWO_PI


def swap(value, axis, size, bit):
    return lax.ppermute(value, axis, [(i, i ^ bit) for i in range(size)])


def powers(size):
    return [1 << k for k in range(size.bit_length() - 1)]


def call(kernel, outs, ins, scratch=(), flops=0, limit=8):
    shapes = [jax.ShapeDtypeStruct(s, d) for s, d in outs]
    moved = sum(math.prod(v.shape) * v.dtype.itemsize for v in [*ins, *shapes])
    return pl.pallas_call(
        kernel,
        out_shape=shapes,
        scratch_shapes=[pltpu.VMEM(s, d) for s, d in scratch],
        compiler_params=pltpu.CompilerParams(vmem_limit_bytes=limit * 1024 * 1024),
        cost_estimate=pl.CostEstimate(flops=flops, bytes_accessed=moved, transcendentals=0),
    )(*ins)


def bit_of(axis, bit):
    return jnp.where((lax.axis_index(axis) & bit) != 0, 1, 0).astype(jnp.int32)


def pack_kernel(wq, wu, pos, g1, b1, g2, b2, bo, bd, bq, q0, q1, q2, q3, u0, u1, u2, u3, small, scr):
    me = lax.axis_index("shard")
    rows = wq.shape[0]
    count = pos.shape[1]
    for k, ref in enumerate((g1, b1, g2, b2, bo, bd)):
        small[k : k + 1, :rows] = as_float(ref[...]).reshape(1, rows)
    small[6:7, : 3 * rows] = as_float(bq[...]).reshape(1, 3 * rows)
    small[7:8, :count] = as_float(pos[...])
    width = wq.shape[1] // 3
    wide = u0.shape[1]
    n_h = rows // HEAD_DIM
    for t in range(4):
        base = rows * t
        for h in range(n_h):
            a = base + HEAD_DIM * h
            scr[t, :, 2 * HEAD_DIM * h : 2 * HEAD_DIM * h + HEAD_DIM] = wq[:, a : a + HEAD_DIM]
            scr[t, :, 2 * HEAD_DIM * h + HEAD_DIM : 2 * HEAD_DIM * (h + 1)] = wq[
                :, width + a : width + a + HEAD_DIM
            ]
        scr[t, :, 2 * rows : 3 * rows] = wq[:, 2 * width + base : 2 * width + base + rows]
    half = q2.shape[0]
    mine = pl.ds(pl.multiple_of(bit_of("rep", 1) * half, 16), half)
    for k, (q, u) in enumerate(((q0, u0), (q1, u1), (q2, u2), (q3, u3))):
        t = me ^ k
        q[...] = scr[t] if k < 2 else scr[t, mine, :]
        u[...] = wu[:, pl.ds(pl.multiple_of(t * wide, 128), wide)]


def normed_of(ref):
    return normalize(ref[...].astype(F32))[0]


def write_rows(targets, grid, first, second, place):
    for target, half, b in zip(
        targets, (1 - first, 1 - first, first, first), (1 - second, second, 1 - second, second)
    ):
        n_t, n_r, _ = target.shape
        for t in range(n_t):
            start = pl.multiple_of(place(half, b, t), 16)
            target[t] = grid[pl.ds(start, n_r), :]


def prep_kernel(x0, x1, x2, x3, c0, c1, c2, c3, s0, s1, s2, s3, wd, wo,
                hid1, hid1_t, hid2, hid2_t, cot, dact, datt, csum, vec, bq_own, sm, bq):
    me = lax.axis_index("shard")
    count = x0.shape[0]
    rows = wo.shape[0]
    width = wo.shape[1]
    for j, ref in enumerate((s0, s1, s2, s3)):
        sm[me ^ j] = ref[...]
    vec[...] = jnp.zeros_like(vec)
    for s in range(4):
        for k in range(6):
            vec[k : k + 1, rows * s : rows * (s + 1)] = sm[s, k : k + 1, :rows]
        bq[:, 3 * rows * s : 3 * rows * (s + 1)] = sm[s, 6:7, :]
    for t in range(4):

        @pl.when(me == t)
        def _(t=t):
            for part in range(3):
                for h in range(rows // HEAD_DIM):
                    a = part * width + rows * t + HEAD_DIM * h
                    b = HEAD_DIM * (2 * h + part) if part < 2 else 2 * rows + HEAD_DIM * h
                    bq_own[:, b : b + HEAD_DIM] = bq[:, a : a + HEAD_DIM]

    gain1, bias1, gain2, bias2 = (vec[k : k + 1, :] for k in range(4))
    for j, (x, c) in enumerate(((x0, c0), (x1, c1), (x2, c2), (x3, c3))):
        place = pl.ds(pl.multiple_of((me ^ j) * count, count), count)
        normed = normed_of(x)
        hid1[place, :] = (normed * gain1 + bias1).astype(BF)
        hid2[place, :] = (normed * gain2 + bias2).astype(BF)
        cot[place, :] = c[...]
    hid1_t[...] = hid1[...].T
    hid2_t[...] = hid2[...].T
    dact[...] = dot(cot[...], wd[...], ((1,), (1,)))
    datt[...] = dot(cot[...], wo[...], ((1,), (1,))).astype(BF)
    csum[...] = jnp.sum(as_float(cot[...]), axis=0, keepdims=True)


def mask_kernel(segc, segr, s0, s1, s2, s3, neg, ca, sa, sb):
    me = lax.axis_index("shard")
    col = lax.broadcasted_iota(jnp.int32, neg.shape, 1)
    row = lax.broadcasted_iota(jnp.int32, neg.shape, 0)
    neg[...] = jnp.where((col <= row) & (segc[...] == segr[...]), 0.0, -jnp.inf)
    count = neg.shape[0] // 4
    half = ROT // 2
    freqs = jnp.exp(
        lax.broadcasted_iota(jnp.int32, (half, count), 0).astype(F32) * (-math.log(10000.0) / half)
    )
    rest = jnp.zeros((HEAD_DIM - ROT, count), F32)
    none = jnp.zeros((half, count), F32)
    for j, ref in enumerate((s0, s1, s2, s3)):
        place = pl.ds(pl.multiple_of((me ^ j) * count, count), count)
        angles = ref[7:8, :count] * freqs
        cosine, sine = jnp.cos(angles), jnp.sin(angles)
        for out, parts in (
            (ca, [cosine, cosine, rest + 1.0]),
            (sa, [-sine, none, rest]),
            (sb, [none, sine, rest]),
        ):
            out[place, :] = jnp.concatenate(parts + parts, axis=0).T


def att_kernel(order, hid, hid_t, cot, datt, q0, q1, q2, q2r, q3, q3r, bq, ca, sa, sb, neg,
               sa_o, sb_o, ka_o, kb_o, att_o, dproj_o, wfull, bsum, grid):
    me = lax.axis_index("shard")
    first, second = (bit_of("rep", bit) for bit in order)
    rows = q0.shape[0]
    _, width = cot.shape
    two = 2 * HEAD_DIM
    n_h = rows // HEAD_DIM
    side = bit_of("rep", 1)
    for j, part, q in ((0, 0, q0), (1, 0, q1), (2, side, q2), (2, 1 - side, q2r), (3, side, q3), (3, 1 - side, q3r)):
        n = q.shape[0]
        wfull[pl.ds(pl.multiple_of((me ^ j) * rows + part * n, 16), n), :] = q[...]
    proj = dot(hid[...], wfull[...], ((1,), (0,))) + bq[...]
    for h in range(n_h):
        qk = proj[:, two * h : two * (h + 1)]
        qk = qk * ca[...] + pltpu.roll(qk, two - ROT // 2, 1) * sa[...] + pltpu.roll(qk, ROT // 2, 1) * sb[...]
        qk = qk.astype(BF)
        query, key = qk[:, :HEAD_DIM], qk[:, HEAD_DIM:]
        vals = slice(2 * rows + HEAD_DIM * h, 2 * rows + HEAD_DIM * (h + 1))
        val = proj[:, vals].astype(BF)
        da = datt[:, HEAD_DIM * h : HEAD_DIM * (h + 1)]
        scores = dot(query * jnp.asarray(0.125, BF), key, ((1,), (1,))) + neg[...]
        top = jnp.max(scores, axis=-1, keepdims=True)
        expo = jnp.exp(scores - top)
        prob = expo * (1.0 / jnp.sum(expo, axis=-1, keepdims=True))
        prob_b = prob.astype(BF)
        att = dot(prob_b, val, ((1,), (0,))).astype(BF)
        att_o[:, HEAD_DIM * h : HEAD_DIM * (h + 1)] = att
        d_val = dot(prob_b, da, ((0,), (0,)))
        d_prob = dot(da, val, ((1,), (1,)))
        row_dot = jnp.sum(as_float(da) * as_float(att), axis=-1, keepdims=True)
        d_score = (prob * (d_prob - row_dot)).astype(BF)
        dqk = 0.125 * jnp.concatenate(
            [dot(d_score, key, ((1,), (0,))), dot(d_score, query, ((0,), (0,)))], axis=1
        )
        dqk = dqk * ca[...] - pltpu.roll(dqk, two - ROT // 2, 1) * sa[...] - pltpu.roll(dqk, ROT // 2, 1) * sb[...]
        dproj_o[:, two * h : two * (h + 1)] = dqk.astype(BF)
        dproj_o[:, vals] = d_val.astype(BF)
        bsum[:, two * h : two * (h + 1)] = jnp.sum(dqk, axis=0, keepdims=True)
        bsum[:, vals] = jnp.sum(d_val, axis=0, keepdims=True)
    grid[:, : 3 * rows] = dot(hid_t[...], dproj_o[...], ((1,), (0,))).astype(BF)
    g_out = dot(att_o[...], cot[...], ((0,), (0,))).astype(BF)
    for t in range(width // rows):
        grid[rows * t : rows * (t + 1), 3 * rows :] = g_out[:, rows * t : rows * (t + 1)]
    n_r = sa_o.shape[1]
    write_rows(
        (sa_o, sb_o, ka_o, kb_o), grid, first, second, lambda half, b, t: t * rows + (2 * half + b) * n_r
    )


def mlp1_kernel(order, hid, cot, u0, u1, u2, u3, bup, sa_o, sb_o, ka_o, kb_o, activ, slope, wfull, grid):
    me = lax.axis_index("shard")
    first, second = (bit_of("rep", bit) for bit in order)
    rows = u0.shape[0]
    for j, u in enumerate((u0, u1, u2, u3)):
        wfull[pl.ds(pl.multiple_of((me ^ j) * rows, 16), rows), :] = u[...]
    block = hid.shape[0] // 4
    for j in range(4):
        part = slice(block * j, block * (j + 1))
        pre_act = dot(hid[part, :], wfull[...], ((1,), (0,))) + bup[...]
        act, slp = gelu_parts(pre_act)
        activ[part, :] = act.astype(BF)
        slope[part, :] = slp
    grid[...] = dot(activ[...], cot[...], ((0,), (0,))).astype(BF)
    n_t, n_r, _ = sa_o.shape
    write_rows(
        (sa_o, sb_o, ka_o, kb_o), grid, first, second, lambda half, b, t: ((half * 2 + b) * n_t + t) * n_r
    )


def mlp2_kernel(order, dact, hid_t, slope, sa_o, sb_o, ka_o, kb_o, dpre, bsum, grid):
    first, second = (bit_of("rep", bit) for bit in order)
    d_pre = dact[...] * slope[...]
    dpre[...] = d_pre.astype(BF)
    bsum[...] = jnp.sum(d_pre, axis=0, keepdims=True)
    grid[...] = dot(hid_t[...], dpre[...], ((1,), (0,))).astype(BF)
    n_r = sa_o.shape[1]
    rows = n_r * 4
    write_rows(
        (sa_o, sb_o, ka_o, kb_o), grid, first, second, lambda half, b, t: t * rows + (2 * half + b) * n_r
    )


def mlp3_kernel(x0, x1, x2, x3, att, activ, dproj, dpre, wo, wd, wq, wu, vec,
                bsum, csum, bup, send, keep, vecs, out_s, one_s, two_s):
    me = lax.axis_index("shard")
    count = x0.shape[0]
    total = [None] * 4
    out_s[...] = dot(att[...], wo[...], ((1,), (0,))) + dot(activ[...], wd[...], ((1,), (0,)))
    one_s[...] = dot(dproj[...], wq[...], ((1,), (1,)))
    two_s[...] = dot(dpre[...], wu[...], ((1,), (1,)))
    for j, x in enumerate((x0, x1, x2, x3)):
        part = pl.ds(pl.multiple_of((me ^ j) * count, count), count)
        out, one, two = out_s[part, :], one_s[part, :], two_s[part, :]
        normed = normed_of(x)
        target = keep if j % 2 == 0 else send
        target[j // 2, :count, :] = out.astype(BF)
        target[j // 2, count : 2 * count, :] = (one * vec[0:1, :] + two * vec[2:3, :]).astype(BF)
        for k, value in enumerate((one * normed, one, two * normed, two)):
            piece = jnp.sum(value, axis=0, keepdims=True)
            total[k] = piece if total[k] is None else total[k] + piece
    rows, _ = wo.shape
    n_h = rows // HEAD_DIM
    vecs[...] = jnp.zeros_like(vecs)
    for t in range(4):
        for k in range(4):
            vecs[t, 0:1, rows * k : rows * (k + 1)] = total[k][:, rows * t : rows * (t + 1)]

        @pl.when(me == t)
        def _(t=t):
            for part in range(3):
                owner, slot = divmod(4 * part + t, 3)
                for h in range(n_h):
                    a = HEAD_DIM * (2 * h + part) if part < 2 else 2 * rows + HEAD_DIM * h
                    b = rows * slot + HEAD_DIM * h
                    vecs[owner, 1:2, b : b + HEAD_DIM] = bsum[:, a : a + HEAD_DIM]
            vecs[t, 1:2, 3 * rows : 4 * rows] = csum[:, rows * t : rows * (t + 1)]
            vecs[t, 2:3, :] = bup[...]

    for j in range(4):
        target = keep if j % 2 == 0 else send
        target[j // 2, 2 * count :, :] = vecs[me ^ j].astype(BF)


def add_kernel(kept, got, out):
    out[...] = (as_float(kept[...]) + as_float(got[...])).astype(out.dtype)


def add_one_kernel(kept, got, out):
    out[...] = (as_float(kept[1]) + as_float(got[1])).astype(BF)


def add_split_kernel(bit, kept, got, more, send, keep):
    mine = bit_of("rep", bit)
    for place, out in ((1 - mine, send), (mine, keep)):
        out[...] = (as_float(kept[place]) + as_float(got[place]) + as_float(more[place])).astype(BF)


def add_pieces_kernel(kept, got, more, p0, p1, p2, p3, *rest):
    me = lax.axis_index("shard")
    cols = p0.shape[1]
    for k, p in enumerate((p0, p1, p2, p3)):
        t = me ^ k
        total = (as_float(kept[t]) + as_float(got[t]) + as_float(more[t])).astype(BF)
        p[...] = total[:, :cols]
        if rest:
            rest[0][t] = total[:, cols:]


def pieces_split_kernel(bit, p0, p1, p2, p3, *rest):
    me = lax.axis_index("shard")
    mine = bit_of("rep", bit)
    send, keep = rest[-2:]
    cols = p0.shape[1]
    for k, p in enumerate((p0, p1, p2, p3)):
        s = me ^ k
        pair, slot = s >> 1, s & 1
        for target, wanted in ((keep, mine), (send, 1 - mine)):

            @pl.when(pair == wanted)
            def _(target=target):
                target[slot, :, :cols] = p[...]
                if len(rest) > 2:
                    target[slot, :, cols:] = rest[0][s]


def last_kernel(kept, got, vec, out):
    n, n_r, _ = kept.shape
    for k in range(n):
        out[n_r * k : n_r * (k + 1), :] = (as_float(kept[k]) + as_float(got[k])).astype(BF)
    out[n_r * n :, :] = vec[...]


def pair_vec_kernel(bit, own, got, out):
    mine = bit_of("rep", bit)
    n = (out.shape[0] - own.shape[0])
    out[pl.ds(pl.multiple_of(mine * n, 16), n), :] = own[:n, :]
    out[pl.ds(pl.multiple_of((1 - mine) * n, 16), n), :] = got[:n, :]
    out[2 * n :, :] = (as_float(own[n:, :]) + as_float(got[n:, :])).astype(BF)


def pair_kernel(bit, own, got, out):
    mine = bit_of("rep", bit)
    out[mine] = own[...]
    out[1 - mine] = got[...]


def quarters(order, refs):
    first, second = (bit_of("rep", bit) for bit in order)
    return zip(refs, (first, first, 1 - first, 1 - first), (second, 1 - second, second, 1 - second))


def final_down_kernel(order, p0, p1, p2, p3, out):
    for value, half, b in quarters(order, (p0, p1, p2, p3)):
        n_t, n_r, _ = value.shape
        for t in range(n_t):
            start = pl.multiple_of(((half * 2 + b) * n_t + t) * n_r, 8)
            out[pl.ds(start, n_r), :] = as_float(value[t])


def final_up_kernel(order, p0, p1, p2, p3, out, g1, b1, g2, b2, tot_q, cot_a, cot_b, tot_u, vec):
    n_r = out.shape[0] // 4
    wide = out.shape[1] // 4
    v0, v1, v2, v3 = (as_float(p[4 * n_r :, :]) for p in (p0, p1, p2, p3))
    vec[...] = (v0 + v1) + (v2 + v3)
    rows = g1.shape[0]
    for k, ref in enumerate((g1, b1, g2, b2)):
        ref[...] = vec[0, rows * k : rows * (k + 1)]
    tot_q[...] = vec[1, : 3 * rows]
    cot_a[...] = vec[1, 3 * rows :]
    cot_b[...] = vec[1, 3 * rows :]
    tot_u[...] = vec[2, :]
    for value, half, b in quarters(order, (p0, p1, p2, p3)):
        start = pl.multiple_of((half * 2 + b) * n_r, 8)
        for s in range(4):
            out[pl.ds(start, n_r), wide * s : wide * (s + 1)] = as_float(value[n_r * s : n_r * (s + 1), :])


def final_qkv_kernel(order, p0, p1, p2, p3, out, out_w):
    rows = out_w.shape[0]
    n_h = rows // HEAD_DIM
    for value, half, b in quarters(order, (p0, p1, p2, p3)):
        n_s, n_r, width = value.shape
        place = pl.ds(pl.multiple_of((half * 2 + b) * n_r, 8), n_r)
        for s in range(n_s):
            block = as_float(value[s])
            for h in range(n_h):
                a = rows * s + HEAD_DIM * h
                two = 2 * HEAD_DIM * h
                out[place, a : a + HEAD_DIM] = block[:, two : two + HEAD_DIM]
                out[place, width + a : width + a + HEAD_DIM] = block[:, two + HEAD_DIM : two + 2 * HEAD_DIM]
            out[place, 2 * width + rows * s : 2 * width + rows * (s + 1)] = block[:, 2 * rows : 3 * rows]
            out_w[place, rows * s : rows * (s + 1)] = block[:, 3 * rows :]


def make_body(shards, reps):
    def body(
        block_input,
        positions,
        segments,
        w_qkv,
        b_qkv,
        w_out,
        b_out,
        w_up,
        b_up,
        w_down,
        b_down,
        ln1_gain,
        ln1_bias,
        ln2_gain,
        ln2_bias,
        cotangent,
    ):
        tokens_in = block_input[0]
        cotan_own = cotangent[0]
        count, width = tokens_in.shape
        length = segments.shape[1]
        rows = w_qkv.shape[0]
        wide = w_up.shape[1] // shards
        bits = powers(reps)

        def to(j, value):
            return swap(value, "shard", shards, j)

        def gather(value):
            two = to(2, value)
            one = to(1, value)
            return value, one, two, swap(two, "shard", shards, 1)

        x = gather(tokens_in)
        packed = call(
            pack_kernel,
            [((rows, 3 * rows), BF)] * 2
            + [((rows // 2, 3 * rows), BF)] * 2
            + [((rows, wide), BF)] * 4
            + [((8, 3 * rows), F32)],
            (w_qkv, w_up, positions, ln1_gain, ln1_bias, ln2_gain, ln2_bias, b_out, b_down, b_qkv),
            scratch=[((4, rows, 3 * rows), BF)],
            limit=62,
        )
        q_two, q_three = to(2, packed[2]), to(3, packed[3])
        q_w = (packed[0], to(1, packed[1]), q_two, swap(q_two, "rep", reps, 1), q_three, swap(q_three, "rep", reps, 1))
        c = gather(cotan_own)
        u_w = (packed[4], *(to(j, packed[4 + j]) for j in (1, 2, 3)))

        small = gather(packed[8])
        first, second, third = bits[:3]
        order_att, order_down, order_up = (first, second), (second, first), (first, second)
        sub = rows // 4
        n_c = width // rows

        hid1, hid1_t, hid2, hid2_t, cot, dact, datt, csum, vec_in, bias_qkv = call(
            prep_kernel,
            [((length, width), BF), ((width, length), BF)] * 2
            + [((length, width), BF), ((length, wide), F32), ((length, rows), BF), ((1, width), F32)]
            + [((8, width), F32), ((1, 3 * rows), F32)],
            (*x, *c, *small, w_down, w_out),
            scratch=[((4, 8, 3 * rows), F32), ((1, 3 * width), F32)],
            flops=1_000_000_000,
            limit=24,
        )
        *grad_a, activ, slope, wu_full = call(
            lambda *refs: mlp1_kernel(order_down, *refs),
            [((2, wide // 8, width), BF)] * 4
            + [((length, wide), BF), ((length, wide), F32), ((width, wide), BF)],
            (hid2, cot, *u_w, as_float(b_up).reshape(1, -1)),
            scratch=[((wide, width), BF)],
            flops=2_000_000_000,
            limit=24,
        )
        *grad_b, dpre, bup_sum = call(
            lambda *refs: mlp2_kernel(order_up, *refs),
            [((shards, sub, wide), BF)] * 4 + [((length, wide), BF), ((1, wide), F32)],
            (dact, hid2_t, slope),
            scratch=[((width, wide), BF)],
            flops=2_000_000_000,
            limit=24,
        )
        neg, ca, sa, sb = call(
            mask_kernel,
            [((length, length), F32)] + [((length, 2 * HEAD_DIM), F32)] * 3,
            (segments.reshape(-1, 1), segments, *small),
            limit=16,
        )
        *grad_c, att, dproj, wq_full, bsum = call(
            lambda *refs: att_kernel(order_att, *refs),
            [((n_c, sub, width), BF)] * 4
            + [
                ((length, rows), BF),
                ((length, 3 * rows), BF),
                ((width, 3 * rows), BF),
                ((1, 3 * rows), F32),
            ],
            (hid1, hid1_t, cot, datt, *q_w, bias_qkv, ca, sa, sb, neg),
            scratch=[((width, width), BF)],
            flops=4_000_000_000,
            limit=24,
        )
        rs_send, rs_keep = call(
            mlp3_kernel,
            [((2, 2 * count + 16, width), BF)] * 2,
            (*x, att, activ, dproj, dpre, w_out, w_down, wq_full, wu_full, vec_in,
             bsum, csum, bup_sum),
            scratch=[((4, 16, width), F32)] + [((length, width), F32)] * 3,
            flops=3_000_000_000,
            limit=24,
        )

        def over(bit, value):
            return swap(value, "rep", reps, bit)

        got = to(1, rs_send)
        (onward,) = call(add_one_kernel, [(got.shape[1:], BF)], (rs_keep, got))
        total = as_float(rs_keep[0]) + as_float(got[0]) + as_float(to(2, onward))
        output = as_float(tokens_in) + total[:count] + vec_in[4:5] + vec_in[5:6]
        d_norm = total[count : 2 * count]
        vec_own = total[2 * count :].astype(BF)
        own_normed, inv_std = normalize(as_float(tokens_in))
        d_input = as_float(cotan_own) + inv_std * (
            d_norm
            - jnp.mean(d_norm, axis=-1, keepdims=True)
            - own_normed * jnp.mean(d_norm * own_normed, axis=-1, keepdims=True)
        )

        def start_sum(bit_order, grad):
            sent_a, sent_b, kept_a, kept_b = grad
            one, two = bit_order
            got_a = over(one, sent_a)
            got_b = over(one, sent_b)
            (sent,) = call(add_kernel, [(kept_a.shape, BF)], (kept_a, got_a))
            return kept_b, got_b, over(two, sent)

        def finish_sum(bit_order, sent, kept, shape, vec=None):
            one, two = bit_order
            got = over(third, sent)
            if vec is None:
                (own,) = call(add_kernel, [(kept.shape, BF)], (kept, got))
            else:
                n_rows = kept.shape[0] * kept.shape[1]
                shape = (2 * n_rows + vec.shape[0], shape[2])
                (own,) = call(last_kernel, [((n_rows + vec.shape[0], shape[1]), BF)], (kept, got, vec))
            for bit in bits[3:]:
                more = over(bit, own)
                (own,) = call(add_kernel, [(own.shape, BF)], (own, more))
            (both,) = call(
                lambda *refs: (pair_kernel if vec is None else pair_vec_kernel)(third, *refs),
                [((2, *own.shape) if vec is None else shape, BF)],
                (own, over(third, own)),
            )
            both = both.reshape(shape)
            other = over(two, both)
            return both, other, over(one, both), over(one, other)

        def shard_stream(bit_order, grad, cols, vec=None):
            held = start_sum(bit_order, grad)
            shape = held[0].shape
            extra = [] if cols == shape[2] else [((n_c, sub, shape[2] - cols), BF)]
            parts = call(add_pieces_kernel, [((sub, cols), BF)] * 4 + extra, held)
            mixed = (parts[0], *(to(j, parts[j]) for j in range(1, 4)), *parts[4:])
            sent, kept = call(lambda *refs: pieces_split_kernel(third, *refs), [((2, sub, shape[2]), BF)] * 2, mixed)
            return finish_sum(bit_order, sent, kept, shape, vec)

        def plain_stream(bit_order, grad):
            held = start_sum(bit_order, grad)
            shape = held[0].shape
            sent, kept = call(lambda *refs: add_split_kernel(third, *refs), [(shape[1:], BF)] * 2, held)
            return finish_sum(bit_order, sent, kept, shape)

        own_c = shard_stream(order_att, grad_c, 3 * rows)
        own_a = plain_stream(order_down, grad_a)
        own_b = shard_stream(order_up, grad_b, wide, vec_own)
        tot_qkv, tot_out = call(
            lambda *refs: final_qkv_kernel(order_att, *refs), [((rows, 3 * width), F32), ((rows, width), F32)], own_c
        )
        (tot_down,) = call(lambda *refs: final_down_kernel(order_down, *refs), [((wide, width), F32)], own_a)
        tot_up, g1, bb1, g2, bb2, tot_bqkv, tot_cot, tot_cot_two, tot_bup = call(
            lambda *refs: final_up_kernel(order_up, *refs),
            [((rows, shards * wide), F32)]
            + [((n,), F32) for n in (rows, rows, rows, rows, 3 * rows, rows, rows, wide)],
            own_b,
            scratch=[(vec_own.shape, F32)],
        )

        return (
            output[None],
            d_input[None],
            tot_qkv,
            tot_bqkv,
            tot_out,
            tot_cot,
            tot_up,
            tot_bup,
            tot_down,
            tot_cot_two,
            g1,
            bb1,
            g2,
            bb2,
        )

    return body


def solution(mesh):
    body = make_body(mesh.shape["shard"], mesh.shape["rep"])
    return jax.shard_map(
        body,
        mesh=mesh,
        in_specs=(
            P("rep", "shard", None),
            P("rep", "shard"),
            P("rep", None),
            P("shard", None),
            P("shard"),
            P("shard", None),
            P("shard"),
            P("shard", None),
            P("shard"),
            P("shard", None),
            P("shard"),
            P("shard"),
            P("shard"),
            P("shard"),
            P("shard"),
            P("rep", "shard", None),
        ),
        out_specs=(
            P("rep", "shard", None),
            P("rep", "shard", None),
            P("shard", None),
            P("shard"),
            P("shard", None),
            P("shard"),
            P("shard", None),
            P("shard"),
            P("shard", None),
            P("shard"),
            P("shard"),
            P("shard"),
            P("shard"),
            P("shard"),
        ),
        check_vma=False,
    )
```
